256 devices in a mesh: row: 32 (over y, x, core), col: 8 (over z).
Axes of the slice: x: 4, y: 4, z: 8, core: 2. Of those that a mesh axis runs over, the one named last changes fastest.
Arguments:
- matrix: float32 [20480, 16384], P('row', 'col'), may hold values from -100 to 100
- pivots: int32 [256], replicated, may hold values from 0 to 16383, as said below
- sketch: float32 [264, 16384], P(None, ('col', 'row')), may hold values from -6 to 6
Outputs:
- upper_rows: float32 [256, 16384], P(None, ('col', 'row'))
- trailing: float32 [20480, 16384], P('row', 'col')
- new_sketch: float32 [264, 16384], P(None, ('col', 'row'))
The draws below stay inside these ranges and needn't reach their ends.
Inputs may be any that keep to these rules, and one draw needn't show every extreme that they name: `pivots`: 256 distinct column indices.
All inputs are finite; a program needn't handle non-finite values.
Results may differ from the reference program's by a relative error of at most 0.0003.
Values sent between devices are 32-bit elements; how exact they have to be, the bound alone decides.
No kernel may reach another device: no remote copies, remote signals or barrier semaphores. Data moves between devices by JAX's collectives and lax.ppermute only.
A program may use at most 128 MiB of HBM per device.

```python
import math
import jax
import jax.numpy as jnp
from jax import lax

BLOCK_COLUMNS = 256
SK = 264
COLUMNS_PER_SHARD = 2048
ROWS = 20480
MATRIX_COLUMNS = 16384


def draw_matrix(key, part):
    keys = jax.random.split(jax.random.fold_in(key, 11), 6)
    along = jnp.arange(ROWS, dtype=jnp.float32) / (ROWS - 1)
    shared = jnp.clip(jax.random.normal(keys[3], (ROWS, 2), jnp.float32), -3.0, 3.0)
    noise = jnp.clip(jax.random.normal(keys[0], (ROWS, MATRIX_COLUMNS), jnp.float32), -5.0, 5.0)
    leading = jax.random.uniform(keys[4], (1, MATRIX_COLUMNS), jnp.float32, 0.1, 0.2)
    row_spread = 0.5
    second = jax.random.uniform(keys[5], (1, MATRIX_COLUMNS), jnp.float32, -0.1, 0.1)
    values = (noise + shared[:, 0:1] * leading + shared[:, 1:2] * second) / math.sqrt(ROWS)
    rough_rows = jax.random.uniform(keys[1], (ROWS,), jnp.float32, -row_spread, row_spread)
    rows_scale = 3.0 ** (along - 0.5) * 10.0 ** rough_rows
    col_scale = 10.0 ** jax.random.uniform(keys[2], (MATRIX_COLUMNS,), jnp.float32, -0.3, 0.3)
    return (values * rows_scale[:, None] * col_scale[None, :]).astype(jnp.float32)


def draw_pivots(key, part):
    keys = jax.random.split(jax.random.fold_in(key, 23), 2)
    column_position = jnp.arange(MATRIX_COLUMNS, dtype=jnp.int32)
    ranking_levels = jax.random.randint(keys[0], (MATRIX_COLUMNS // COLUMNS_PER_SHARD,), 0, 3).astype(jnp.int32)
    starting_column = jax.random.permutation(keys[1], MATRIX_COLUMNS).astype(jnp.int32)
    priority_boost = ranking_levels[column_position // COLUMNS_PER_SHARD] * (MATRIX_COLUMNS // 4) + (column_position < BLOCK_COLUMNS).astype(jnp.int32) * (MATRIX_COLUMNS // 4)
    ends_boost = ((column_position == 0) | (column_position == MATRIX_COLUMNS - 1)).astype(jnp.int32) * (2 * MATRIX_COLUMNS)
    column_scores = (starting_column + priority_boost + ends_boost) * MATRIX_COLUMNS + column_position
    ranked, chosen = lax.top_k(column_scores, BLOCK_COLUMNS)
    return chosen.astype(jnp.int32)


def block_scale(stream_key, extent, pieces, smallest, largest):
    level, own = 1.0, jax.random.fold_in(stream_key, 6)
    for position, blocks in pieces:
        steps = jnp.exp(jax.random.uniform(jax.random.fold_in(own, position), (blocks,), jnp.float32, smallest / len(pieces), largest / len(pieces)))
        level = level * jnp.repeat(steps, extent[position] // blocks).reshape([-1 if axis == position else 1 for axis in range(len(extent))])
    return level


def centred(stream_key, shape, deviation, reach, shards=(), held_as=jnp.bfloat16):
    gain = block_scale(stream_key, shape, shards, -0.22, 0.18) if shards else 1.0
    result = jax.random.normal(stream_key, shape, jnp.float32) * deviation * gain
    return jnp.minimum(jnp.maximum(result, -reach), reach).astype(held_as)


def setup_inputs(seed: int = 0) -> dict:
    splits = jax.random.split(jax.random.key(seed), 4)
    matrix = draw_matrix(jax.random.fold_in(splits[3], 71), 0)
    pivots = draw_pivots(jax.random.fold_in(splits[3], 71), 0)
    sketch = centred(splits[2], (SK, MATRIX_COLUMNS), 1.0, 6.0, ((1, 256),), jnp.float32)
    return dict(matrix=matrix, pivots=pivots, sketch=sketch)


sentinel_value = 1 << 30
highest = lax.Precision.HIGHEST

def pairing(pivots, panel_cols):
    positions = jnp.arange(panel_cols, dtype=jnp.int32)
    present = jnp.any(pivots[None, :] == positions[:, None], axis=1)
    displaced = jnp.sort(jnp.where(present, sentinel_value, positions).astype(jnp.int32))
    vacated = jnp.sort(jnp.where(pivots >= panel_cols, pivots, sentinel_value).astype(jnp.int32))
    return (vacated, displaced)

def reference(matrix, pivots, sketch):
    vacated, displaced = pairing(pivots, BLOCK_COLUMNS)
    order = jnp.arange(MATRIX_COLUMNS, dtype=jnp.int32)
    order = order.at[vacated].set(displaced, mode='drop')
    order = order.at[:BLOCK_COLUMNS].set(pivots.astype(jnp.int32))
    permuted = jnp.take(matrix, order, axis=1)
    panel = permuted[:, :BLOCK_COLUMNS]
    basis, upper = jnp.linalg.qr(panel)
    signs = jnp.sign(jnp.diagonal(upper))
    basis = basis * signs[None, :]
    upper = upper * signs[:, None]
    upper_rows = jnp.dot(basis.T.astype(jnp.float32), permuted.astype(jnp.float32), precision=highest, preferred_element_type=jnp.float32)
    trailing = permuted - jnp.dot(basis.astype(jnp.float32), upper_rows.astype(jnp.float32), precision=highest, preferred_element_type=jnp.float32)
    moved = jnp.take(sketch, order, axis=1)
    solved = lax.linalg.triangular_solve(upper, upper_rows, left_side=True, lower=False)
    new_sketch = moved - jnp.dot(moved[:, :BLOCK_COLUMNS].astype(jnp.float32), solved.astype(jnp.float32), precision=highest, preferred_element_type=jnp.float32)
    return (upper_rows, trailing, new_sketch)
```

```python
import functools

import jax
import jax.numpy as jnp
from jax import lax
from jax.experimental import pallas as pl
from jax.experimental.pallas import tpu as pltpu
from jax.sharding import Mesh
from jax.sharding import PartitionSpec as P

ROW = ("row_0", "row_1", "row_2")
CHIPS = ("row_0", "row_1")
COL_ROW = ("col", "row_0", "row_1", "row_2")

f32, bf16, i32 = jnp.float32, jnp.bfloat16, jnp.int32
highest = lax.Precision.HIGHEST
NN = (((1,), (0,)), ((), ()))
NT = (((1,), (1,)), ((), ()))
TN = (((0,), (0,)), ((), ()))


def iota(shape, dim):
    return lax.broadcasted_iota(i32, shape, dim)


def dot(a, b, dims=NN, precision=None):
    return lax.dot_general(a, b, dims, precision=precision, preferred_element_type=f32)


def split(a, pieces):
    out = []
    for _ in range(pieces - 1):
        top = a.astype(bf16)
        out.append(top)
        a = a - top.astype(f32)
    return (*out, a.astype(bf16))


def picked(a, onehot, dims=NN):
    hi, mid, lo = split(a, 3)
    return dot(hi, onehot, dims) + dot(mid, onehot, dims) + dot(lo, onehot, dims)


def partners(prow, pcol):
    n = prow.shape[1]
    drow, dcol = iota((1, n), 1), iota((n, 1), 0)
    gone_col = jnp.max(jnp.where(prow == dcol, 1, 0), axis=1, keepdims=True)
    gone_row = jnp.max(jnp.where(pcol == drow, 1, 0), axis=0, keepdims=True)
    rank_d = jnp.sum(jnp.where(drow < dcol, 1 - gone_row, 0), axis=1, keepdims=True)
    rank_v = jnp.sum(jnp.where((pcol < prow) & (pcol >= n), 1, 0), axis=0, keepdims=True)
    match = (rank_d == rank_v) & (gone_col == 0) & (prow >= n)
    return jnp.sum(jnp.where(match, dcol + 1, 0), axis=0, keepdims=True) - 1


def wanted(prow, partner, c, columns):
    n = prow.shape[1]
    off = c * columns
    own = (prow >= off) & (prow < off + columns)
    sel = jnp.where(own, prow - off, jnp.where(c == 0, partner, -1))
    own_disp = jnp.where(own & (prow >= n) & (c == 0), partner, -1)
    return own, sel, own_disp


def extract_kernel(c_ref, prow_ref, pcol_ref, a_ref, m_ref, d_ref, e_ref, e2_ref):
    columns = a_ref.shape[1]
    n = prow_ref.shape[1]

    @pl.when(pl.program_id(0) == 0)
    def _():
        prow = prow_ref[...]
        _, sel, disp = wanted(prow, partners(prow, pcol_ref[...]), c_ref[0], columns)
        for s in range(0, columns, n):
            e_ref[s : s + n, :] = jnp.where(iota((n, n), 0) + s == sel, 1.0, 0.0).astype(bf16)
        e2_ref[...] = jnp.where(iota((n, n), 0) == disp, 1.0, 0.0).astype(bf16)

    a = a_ref[...]
    m_ref[...] = picked(a, e_ref[...])
    d_ref[...] = picked(a[:, :n], e2_ref[...])


def extract(c, prow, pcol, a):
    rows, columns = a.shape
    n = prow.shape[1]
    tm = 128
    small = lambda shape: pl.BlockSpec(shape, lambda i, *_: (0, 0))
    return pl.pallas_call(
        extract_kernel,
        out_shape=(jax.ShapeDtypeStruct((rows, n), f32),) * 2,
        grid_spec=pltpu.PrefetchScalarGridSpec(
            num_scalar_prefetch=1,
            grid=(rows // tm,),
            in_specs=[small((1, n)), small((n, 1)), pl.BlockSpec((tm, columns), lambda i, *_: (i, 0))],
            out_specs=(pl.BlockSpec((tm, n), lambda i, *_: (i, 0)),) * 2,
            scratch_shapes=[pltpu.VMEM((columns, n), bf16), pltpu.VMEM((n, n), bf16)],
        ),
        name="extract",
    )(c, prow, pcol, a)


def holder_kernel(columns, prow_ref, r_ref, o_ref):
    peers = r_ref.shape[0]
    prow = prow_ref[...]
    owns = [(prow >= s * columns) & (prow < (s + 1) * columns) for s in range(peers)]
    panel = jnp.zeros(r_ref.shape[1:], f32)
    for s in range(peers):
        panel = jnp.where(owns[s], r_ref[s], panel)
    o_ref[0] = panel
    for s in range(1, peers):
        o_ref[s] = jnp.where(owns[s], r_ref[0], panel)


def holder(prow, received, columns):
    return pl.pallas_call(
        functools.partial(holder_kernel, columns),
        out_shape=jax.ShapeDtypeStruct(received.shape, f32),
        name="holder",
    )(prow, received)


def gram_kernel(columns, c_ref, prow_ref, x_ref, m_ref, d0_ref, p_ref, d_ref, g_ref, dp_ref):
    c = c_ref[0]
    prow = prow_ref[...]
    own = (prow >= c * columns) & (prow < (c + 1) * columns)
    x = x_ref[...]
    panel = jnp.where(own, m_ref[...], x)
    moved = jnp.where(c == 0, d0_ref[...], jnp.where(own, x, 0.0))
    p_ref[...] = panel
    d_ref[...] = moved
    g_ref[...] = dot(panel, panel, TN, highest)
    dp_ref[...] = dot(moved, panel, TN, highest)


def gram(c, prow, x, m, d0, columns):
    rows, n = x.shape
    whole = lambda s: pl.BlockSpec(s, lambda *_: (0, 0))
    return pl.pallas_call(
        functools.partial(gram_kernel, columns),
        out_shape=tuple(jax.ShapeDtypeStruct(s, f32) for s in ((rows, n), (rows, n), (n, n), (n, n))),
        grid_spec=pltpu.PrefetchScalarGridSpec(
            num_scalar_prefetch=1,
            grid=(1,),
            in_specs=[whole((1, n))] + [whole((rows, n))] * 3,
            out_specs=tuple(whole(s) for s in ((rows, n), (rows, n), (n, n), (n, n))),
        ),
        name="gram",
    )(c, prow, x, m, d0)


def product_kernel(columns, ck_ref, prow_ref, a_ref, p_ref, g_ref, dp_ref, keep_ref, send_ref, r_ref):
    c, k = ck_ref[0], ck_ref[1]
    b = pl.program_id(0)
    tn = a_ref.shape[1]
    half = tn // 2
    n = prow_ref.shape[1]
    place = c * columns + b * tn + iota((tn, 1), 0)
    onehot = jnp.where(place == prow_ref[...], 1.0, 0.0)
    stays = 1.0 - jnp.max(onehot, axis=1, keepdims=True)
    stays = jnp.where(place < n, 0.0, stays)
    r = dot(a_ref[...], p_ref[...], TN, highest) * stays + dot(onehot, dp_ref[...], NN, highest)
    r_ref[...] = r

    @pl.when((c == 0) & (b < n // tn))
    def _():
        r_ref[...] = g_ref[pl.ds(jnp.minimum(b, n // tn - 1) * tn, tn), :]

    keep_ref[0] = r_ref[pl.ds(k * half, half), :]
    send_ref[0] = r_ref[pl.ds((1 - k) * half, half), :]


def product(ck, prow, a, p, g, dp):
    rows, columns = a.shape
    n = prow.shape[1]
    tn = 128
    whole = lambda s: pl.BlockSpec(s, lambda *_: (0, 0))
    return pl.pallas_call(
        functools.partial(product_kernel, columns),
        out_shape=(jax.ShapeDtypeStruct((columns // tn, tn // 2, n), f32),) * 2,
        grid_spec=pltpu.PrefetchScalarGridSpec(
            num_scalar_prefetch=1,
            grid=(columns // tn,),
            in_specs=[
                whole((1, n)),
                pl.BlockSpec((rows, tn), lambda b, *_: (0, b)),
                whole((rows, n)),
                whole((n, n)),
                whole((n, n)),
            ],
            out_specs=(pl.BlockSpec((1, tn // 2, n), lambda b, *_: (b, 0, 0)),) * 2,
            scratch_shapes=[pltpu.VMEM((tn, n), f32)],
        ),
        name="product",
    )(ck, prow, a, p, g, dp)


def permute_kernel(columns, c_ref, prow_ref, pcol_ref, a_ref, p_ref, d_ref, o_ref):
    c = c_ref[0]
    b = pl.program_id(0)
    tn = a_ref.shape[1]
    n = prow_ref.shape[1]
    start = c * columns + b * tn
    onehot = jnp.where(start + iota((tn, 1), 0) == prow_ref[...], 1.0, 0.0).astype(bf16)
    here = jnp.max(jnp.where(pcol_ref[...] == start + iota((1, tn), 1), 1, 0), axis=0, keepdims=True)
    o_ref[...] = jnp.where(here > 0, picked(d_ref[...], onehot, NT), a_ref[...])
    for s in range(n // tn):

        @pl.when((c == 0) & (b == s))
        def _():
            o_ref[...] = p_ref[:, s * tn : (s + 1) * tn]


def permute(c, prow, pcol, a, p, d):
    rows, columns = a.shape
    n = prow.shape[1]
    tn = 128
    whole = lambda s: pl.BlockSpec(s, lambda *_: (0, 0))
    return pl.pallas_call(
        functools.partial(permute_kernel, columns),
        out_shape=jax.ShapeDtypeStruct(a.shape, f32),
        grid_spec=pltpu.PrefetchScalarGridSpec(
            num_scalar_prefetch=1,
            grid=(columns // tn,),
            in_specs=[
                whole((1, n)),
                whole((n, 1)),
                pl.BlockSpec((rows, tn), lambda b, *_: (0, b)),
                whole((rows, n)),
                whole((rows, n)),
            ],
            out_specs=pl.BlockSpec((rows, tn), lambda b, *_: (0, b)),
        ),
        name="permute",
    )(c, prow, pcol, a, p, d)


def factor_kernel(g_ref, o_ref, t_ref):
    n = g_ref.shape[0]
    nb = 64
    t_ref[:, :n] = g_ref[...]
    t_ref[:, n:] = jnp.where(iota((n, n), 0) == iota((n, n), 1), 1.0, 0.0)
    eye = jnp.where(iota((nb, nb), 0) == iota((nb, nb), 1), 1.0, 0.0)
    below = iota((nb, 1), 0)
    for s in range(0, n, nb):
        t = jnp.concatenate([t_ref[s : s + nb, s : s + nb], eye], axis=1)
        scale = jnp.zeros((nb, 1), f32)
        for j in range(nb):
            row = t[j : j + 1, :]
            pivot = row[:, j : j + 1]
            scale = jnp.where(below == j, lax.rsqrt(pivot), scale)
            if j + 1 < nb:
                scaled = row * (1.0 / pivot)
                mult = jnp.where(below > j, t[:, j : j + 1], 0.0)
                t = t - mult * scaled
        inv = t[:, nb:] * scale
        y = dot(inv, t_ref[s : s + nb, :], NN, highest)
        o_ref[s : s + nb, :] = y[:, n:]
        if s + nb < n:
            t_ref[s + nb :, :] = t_ref[s + nb :, :] - dot(y[:, s + nb : n], y, TN, highest)


def factor(g):
    n = g.shape[0]
    return pl.pallas_call(
        factor_kernel,
        out_shape=jax.ShapeDtypeStruct((n, n), f32),
        scratch_shapes=[pltpu.VMEM((n, 2 * n), f32)],
        name="factor",
    )(g)


def basis_kernel(p_ref, inv_ref, hi_ref, lo_ref):
    hi_ref[...], lo_ref[...] = split(dot(p_ref[...], inv_ref[...], NT, highest), 2)


def basis_of(p, inverse):
    return pl.pallas_call(
        basis_kernel,
        out_shape=(jax.ShapeDtypeStruct(p.shape, bf16),) * 2,
        name="basis",
    )(p, inverse)


def trailing_kernel(k_ref, a_ref, hi_ref, lo_ref, inv_ref, mine_ref, other_ref, o_ref, s_ref):
    k = k_ref[0]
    half = mine_ref.shape[1]
    s_ref[pl.ds(k * half, half), :] = mine_ref[0]
    s_ref[pl.ds((1 - k) * half, half), :] = other_ref[0]
    u_hi, u_lo = split(dot(s_ref[...], inv_ref[...], NT, highest), 2)
    hi, lo = hi_ref[...], lo_ref[...]
    o_ref[...] = a_ref[...] - (dot(hi, u_hi, NT) + (dot(hi, u_lo, NT) + dot(lo, u_hi, NT)))


def trail(k, a, hi, lo, inverse, mine, other):
    rows, columns = a.shape
    blocks, half, n = mine.shape
    tn = 2 * half
    whole = lambda s: pl.BlockSpec(s, lambda *_: (0, 0))
    share = pl.BlockSpec((1, half, n), lambda b, *_: (b, 0, 0))
    return pl.pallas_call(
        trailing_kernel,
        out_shape=jax.ShapeDtypeStruct(a.shape, f32),
        grid_spec=pltpu.PrefetchScalarGridSpec(
            num_scalar_prefetch=1,
            grid=(blocks,),
            in_specs=[
                pl.BlockSpec((rows, tn), lambda b, *_: (0, b)),
                whole((rows, n)),
                whole((rows, n)),
                whole((n, n)),
                share,
                share,
            ],
            out_specs=pl.BlockSpec((rows, tn), lambda b, *_: (0, b)),
            scratch_shapes=[pltpu.VMEM((tn, n), f32)],
        ),
        name="trailing",
    )(k, a, hi, lo, inverse, mine, other)


def exchange(pieces, axis):
    return lax.all_to_all(pieces, axis, split_axis=0, concat_axis=0, tiled=True)


def to_all(piece, axis):
    return exchange(jnp.broadcast_to(piece[None], (lax.axis_size(axis), *piece.shape)), axis)


def per_device(matrix, pivots, sketch):
    c = lax.axis_index("col")
    r = lax.axis_index(ROW)
    k = lax.axis_index("row_2")
    cols, lanes = lax.axis_size("col"), lax.axis_size(ROW)
    rows, columns = matrix.shape
    n = pivots.shape[0]
    prow, pcol = pivots.reshape(1, n), pivots.reshape(n, 1)
    c1 = c.reshape(1).astype(i32)
    k1 = k.reshape(1).astype(i32)
    ck = jnp.stack([c, k]).astype(i32)

    mine, inside = extract(c1, prow, pcol, matrix)
    arrived = exchange(mine.reshape(cols, rows // cols, n), "col")
    x = exchange(holder(prow, arrived, columns), "col").reshape(rows, n)
    panel, displaced, gram_part, moved_part = gram(c1, prow, x, mine, inside, columns)

    gram_own = exchange(gram_part.reshape(lanes, n // lanes, n), ROW).sum(axis=0)
    keep, send = product(ck, prow, matrix, panel, gram_part, moved_part)
    swap = [(0, 1), (1, 0)]
    half = keep + lax.ppermute(send, "row_2", swap)
    share = exchange(half, CHIPS).sum(axis=0)
    own_all = to_all(share, CHIPS)
    gram_all = to_all(gram_own, ROW).reshape(n, n)
    permuted = permute(c1, prow, pcol, matrix, panel, displaced)
    other_all = lax.ppermute(own_all, "row_2", swap)
    inverse = factor(gram_all)
    hi, lo = basis_of(panel, inverse)
    trailing = trail(k1, permuted, hi, lo, inverse, own_all, other_all)
    upper_share = dot(inverse, share, NT, highest)

    pieces = sketch.shape[1]
    size = -(-sketch.shape[0] // lanes)
    padded = jnp.pad(sketch, ((0, size * lanes - sketch.shape[0]), (0, 0)))
    partner = partners(prow, pcol)
    own, sel, disp = wanted(prow, partner, c, columns)
    place = r * pieces + iota((pieces, 1), 0)
    pick = jnp.concatenate([jnp.where(place == sel, 1.0, 0.0), jnp.where(place == disp, 1.0, 0.0)], 1)
    part = dot(padded, pick, NN, highest).reshape(lanes, size, 2 * n)
    line = exchange(part, ROW).sum(axis=0)
    slots, inside_s = line[:, :n], line[:, n:]
    got = to_all(slots, "col")
    owner = [(prow >= s * columns) & (prow < (s + 1) * columns) for s in range(cols)]
    front = functools.reduce(lambda acc, s: jnp.where(owner[s], got[s], acc), range(cols), slots)
    back = jnp.where(c == 0, inside_s, jnp.where(own, got[0], 0.0))
    both = to_all(jnp.concatenate([front, back], 1), ROW).reshape(lanes * size, 2 * n)[: sketch.shape[0]]
    fronts, backs = both[:, :n], both[:, n:]
    glob = c * columns + r * pieces
    hit = jnp.where(glob + iota((pieces, 1), 0) == prow, 1.0, 0.0)
    lead = jnp.where((glob + iota((pieces, 1), 0) == iota((1, n), 1)), 1.0, 0.0)
    stays = (jnp.max(jnp.where(pcol == glob + iota((1, pieces), 1), 1, 0), axis=0, keepdims=True) == 0) & (
        glob + iota((1, pieces), 1) >= n
    )
    moved = jnp.where(stays, sketch, dot(backs, hit, NT, highest) + dot(fronts, lead, NT, highest))
    solved = dot(inverse, upper_share, TN, highest)
    new_sketch = moved - dot(fronts, solved, NN, highest)
    return (upper_share, trailing, new_sketch)


def solution(mesh):
    finer = Mesh(mesh.devices.reshape(4, 4, 2, mesh.shape["col"]), ("row_0", "row_1", "row_2", "col"))
    return jax.shard_map(
        per_device,
        mesh=finer,
        in_specs=(P(ROW, "col"), P(), P(None, COL_ROW)),
        out_specs=(P(None, COL_ROW), P(ROW, "col"), P(None, COL_ROW)),
        check_vma=False,
    )
```

```python
import functools

import jax
import jax.numpy as jnp
from jax import lax
from jax.experimental import pallas as pl
from jax.experimental.pallas import tpu as pltpu
from jax.sharding import Mesh
from jax.sharding import PartitionSpec as P


ROW = ("row_0", "row_1", "row_2")
CHIPS = ("row_0", "row_1")
COL_ROW = ("col", "row_0", "row_1", "row_2")

f32, bf16, i32 = jnp.float32, jnp.bfloat16, jnp.int32
highest = lax.Precision.HIGHEST
NN = (((1,), (0,)), ((), ()))
NT = (((1,), (1,)), ((), ()))
TN = (((0,), (0,)), ((), ()))


def iota(shape, dim):
    return lax.broadcasted_iota(i32, shape, dim)


def dot(a, b, dims=NN, precision=None):
    return lax.dot_general(a, b, dims, precision=precision, preferred_element_type=f32)


def split(a, pieces):
    out = []
    for _ in range(pieces - 1):
        top = a.astype(bf16)
        out.append(top)
        a = a - top.astype(f32)
    return (*out, a.astype(bf16))


def stacked(a):
    return jnp.concatenate(split(a, 2), axis=0)


def folded(top_bottom):
    rows = top_bottom.shape[0] // 2
    return top_bottom[:rows] + top_bottom[rows:]


def product3(left, right):
    hi, lo = split(right, 2)
    return folded(dot(left, hi)) + dot(left[: left.shape[0] // 2], lo)


def owned(place, c, columns):
    return (place >= c * columns) & (place < (c + 1) * columns)


def onehot_rows(pcol, start, width):
    lanes = pcol.shape[1]
    return jnp.concatenate(
        [
            jnp.where(pcol[:, : min(lanes, width - s)] == start + s + iota((1, min(lanes, width - s)), 1), 1.0, 0.0)
            for s in range(0, width, lanes)
        ],
        axis=1,
    )


def whole(shape):
    return pl.BlockSpec(shape, lambda *_: (0,) * len(shape))


def scalars(*values):
    return jnp.stack([jnp.asarray(v, i32) for v in values])


def prepare_kernel(columns, at_ref, prow_ref, sk_ref, partner_ref, pcol_ref, s_ref):
    n = prow_ref.shape[1]
    c, r = at_ref[0], at_ref[2]
    prow = prow_ref[...]
    across = jnp.broadcast_to(prow.astype(f32), (n, n))
    down = across.T.astype(i32)
    pcol_ref[...] = down[:, : pcol_ref.shape[1]]
    named = jnp.where(iota((n, n), 0) == prow, 1.0, 0.0).astype(bf16)
    free = 1.0 - dot(named, jnp.ones((n, n), bf16))
    upto = jnp.where(iota((n, n), 1) <= iota((n, n), 0), 1.0, 0.0).astype(bf16)
    count = dot(upto, free.astype(bf16))
    rank = jnp.sum(jnp.where((down < prow) & (down >= n), 1.0, 0.0), axis=0, keepdims=True)
    partner = jnp.sum(jnp.where(count <= rank, 1.0, 0.0), axis=0, keepdims=True).astype(i32)
    partner = jnp.where(prow >= n, partner, -1)
    partner_ref[...] = partner
    own = owned(prow, c, columns)
    sel = jnp.where(own, prow - c * columns, jnp.where(c == 0, partner, -1))
    disp = jnp.where(own & (c == 0), partner, -1)
    pieces, rows = sk_ref.shape
    lanes, size, _ = s_ref.shape
    place = r * pieces + iota((pieces, 1), 0)
    pick = jnp.concatenate([jnp.where(place == sel, 1.0, 0.0), jnp.where(place == disp, 1.0, 0.0)], axis=1)
    hi, lo = split(sk_ref[...], 2)
    pick = pick.astype(bf16)
    line = dot(hi, pick, TN) + dot(lo, pick, TN)
    for i in range(lanes):
        low, high = min(i * size, rows), min((i + 1) * size, rows)
        if high > low:
            s_ref[i, : high - low, :] = line[low:high, :]
        if high - low < size:
            s_ref[i, high - low :, :] = jnp.zeros((size - (high - low), 2 * n), f32)


def prepare(at, prow, sketch, columns, lanes):
    n = prow.shape[1]
    size = -(-sketch.shape[1] // lanes)
    outs = (((1, n), i32), ((n, 128), i32), ((lanes, size, 2 * n), f32))
    return pl.pallas_call(
        functools.partial(prepare_kernel, columns),
        out_shape=tuple(jax.ShapeDtypeStruct(s, t) for s, t in outs),
        grid_spec=pltpu.PrefetchScalarGridSpec(
            num_scalar_prefetch=1,
            grid=(1,),
            in_specs=[whole((1, n)), whole(sketch.shape)],
            out_specs=tuple(whole(s) for s, _ in outs),
        ),
        name="prepare",
    )(at, prow, sketch)


def extract_kernel(at_ref, prow_ref, partner_ref, a_ref, m_ref, e_ref):
    columns = a_ref.shape[1]
    n = prow_ref.shape[1]
    c = at_ref[0]

    @pl.when(pl.program_id(0) == 0)
    def _():
        prow = prow_ref[...]
        sel = jnp.where(owned(prow, c, columns), prow - c * columns, jnp.where(c == 0, partner_ref[...], -1))
        for s in range(0, columns, n):
            e_ref[s : s + n, :] = jnp.where(iota((n, n), 0) == sel - s, 1.0, 0.0).astype(bf16)

    m_ref[...] = folded(dot(stacked(a_ref[...]), e_ref[...]))


def extract(at, prow, partner, a):
    rows, columns = a.shape
    n = prow.shape[1]
    tm = 128
    return pl.pallas_call(
        extract_kernel,
        out_shape=jax.ShapeDtypeStruct((rows, n), f32),
        grid_spec=pltpu.PrefetchScalarGridSpec(
            num_scalar_prefetch=1,
            grid=(rows // tm,),
            in_specs=[whole((1, n)), whole((1, n)), pl.BlockSpec((tm, columns), lambda i, *_: (i, 0))],
            out_specs=pl.BlockSpec((tm, n), lambda i, *_: (i, 0)),
            scratch_shapes=[pltpu.VMEM((columns, n), bf16)],
        ),
        name="extract",
    )(at, prow, partner, a)


def inside_kernel(columns, at_ref, prow_ref, partner_ref, a_ref, d_ref):
    n = prow_ref.shape[1]
    c = at_ref[0]
    disp = jnp.where(owned(prow_ref[...], c, columns) & (c == 0), partner_ref[...], -1)
    d_ref[...] = folded(dot(stacked(a_ref[...]), jnp.where(iota((n, n), 0) == disp, 1.0, 0.0).astype(bf16)))


def inside_of(at, prow, partner, a):
    rows, columns = a.shape
    n = prow.shape[1]
    return pl.pallas_call(
        functools.partial(inside_kernel, columns),
        out_shape=jax.ShapeDtypeStruct((rows, n), f32),
        grid_spec=pltpu.PrefetchScalarGridSpec(
            num_scalar_prefetch=1,
            grid=(1,),
            in_specs=[whole((1, n)), whole((1, n)), whole((rows, n))],
            out_specs=whole((rows, n)),
        ),
        name="inside",
    )(at, prow, partner, a)


def padded_to(rows, multiple):
    return -(-rows // multiple) * multiple


def holder_kernel(columns, prow_ref, r_ref, line_ref, o_ref):
    peers, height, n = r_ref.shape
    size = line_ref.shape[0]
    prow = prow_ref[...]
    panel = r_ref[0]
    for s in range(1, peers):
        panel = jnp.where(owned(prow, s, columns), r_ref[s], panel)
    line = line_ref[:, :n]
    for s in range(peers):
        o_ref[s, :height] = jnp.where(owned(prow, s, columns), r_ref[0], panel) if s else panel
        o_ref[s, height : height + size] = line
        o_ref[s, height + size :] = jnp.zeros((o_ref.shape[1] - height - size, n), f32)


def holder(prow, received, line, columns):
    peers, height, n = received.shape
    return pl.pallas_call(
        functools.partial(holder_kernel, columns),
        out_shape=jax.ShapeDtypeStruct((peers, padded_to(height + line.shape[0], 8), n), f32),
        name="holder",
    )(prow, received, line)


def gram_kernel(columns, at_ref, prow_ref, x_ref, m_ref, d0_ref, line_ref, p_ref, d_ref, w_ref, g_ref, o_ref, x_s):
    c = at_ref[0]
    peers = x_ref.shape[0]
    rows, n = m_ref.shape
    height = rows // peers
    size = line_ref.shape[0]
    lanes, piece, _ = o_ref.shape
    prow = prow_ref[...]
    own = owned(prow, c, columns)
    for s in range(peers):
        x_s[s * height : (s + 1) * height, :] = x_ref[s, :height]
    x = x_s[...]
    panel = jnp.where(own, m_ref[...], x)
    moved = jnp.where(c == 0, d0_ref[...], jnp.where(own, x, 0.0))
    p_ref[...] = panel
    d_ref[...] = stacked(moved)
    turned = panel.T
    total = dot(turned, panel, NN, highest)
    g_ref[...] = total
    left = stacked(turned)
    w_ref[:, :rows] = left
    w_ref[:, rows:] = stacked(product3(left, moved))
    got = [x_ref[s, height : height + size] for s in range(peers)]
    front = got[0]
    for s in range(1, peers):
        front = jnp.where(owned(prow, s, columns), got[s], front)
    back = jnp.where(c == 0, line_ref[:, n:], got[0])
    part = n // lanes
    share = columns // lanes
    for i in range(lanes):
        o_ref[i, :part] = total[i * part : (i + 1) * part]
        o_ref[i, part : part + size] = jnp.where(owned(prow, c * lanes + i, share), back, front)
        o_ref[i, part + size :] = jnp.zeros((piece - part - size, n), f32)


def gram(at, prow, x, m, d0, line, columns, lanes):
    rows, n = m.shape
    piece = padded_to(n // lanes + line.shape[0], 8)
    outs = (
        ((rows, n), f32),
        ((2 * rows, n), bf16),
        ((2 * n, rows + n), bf16),
        ((n, n), f32),
        ((lanes, piece, n), f32),
    )
    return pl.pallas_call(
        functools.partial(gram_kernel, columns),
        out_shape=tuple(jax.ShapeDtypeStruct(s, t) for s, t in outs),
        grid_spec=pltpu.PrefetchScalarGridSpec(
            num_scalar_prefetch=1,
            grid=(1,),
            in_specs=[whole(v.shape) for v in (prow, x, m, d0, line)],
            out_specs=tuple(whole(s) for s, _ in outs),
            scratch_shapes=[pltpu.VMEM((rows, n), f32)],
        ),
        name="gram",
    )(at, prow, x, m, d0, line)


def half_kernel(part, size, keep_ref, sent_ref, got_ref, o_ref, line_ref):
    chips, half, lanes = keep_ref.shape
    peers, _, n = got_ref.shape
    o_ref[:, :half, :] = keep_ref[...] + sent_ref[...]
    total = got_ref[0, :part]
    for s in range(1, peers):
        total = total + got_ref[s, :part]
    for s in range(chips):
        for t in range(n // lanes):
            o_ref[s, half + t * part : half + (t + 1) * part, :] = total[:, t * lanes : (t + 1) * lanes]

    @pl.when(pl.program_id(0) == 0)
    def _():
        for s in range(peers):
            line_ref[s * size : (s + 1) * size, :] = got_ref[s, part : part + size]


def add_halves(keep, sent, got, size):
    chips, half, lanes = keep.shape
    peers, _, n = got.shape
    part = n // peers
    tall = half + part * (n // lanes)
    step = 4
    block = pl.BlockSpec((step, half, lanes), lambda b: (b, 0, 0))
    return pl.pallas_call(
        functools.partial(half_kernel, part, size),
        out_shape=(
            jax.ShapeDtypeStruct((chips, tall, lanes), f32),
            jax.ShapeDtypeStruct((peers * size, n), f32),
        ),
        grid=(chips // step,),
        in_specs=[block, block, whole(got.shape)],
        out_specs=(pl.BlockSpec((step, tall, lanes), lambda b: (b, 0, 0)), whole((peers * size, n))),
        name="half",
    )(keep, sent, got)


def total_kernel(r_ref, share_ref, o_ref):
    chips, half, _ = o_ref.shape
    extra = r_ref.shape[1] - half
    total = r_ref[0, :half]
    for s in range(1, chips):
        total = total + r_ref[s, :half]
    share_ref[:half, :] = total
    for s in range(chips):
        o_ref[s] = total
        share_ref[half + s * extra : half + (s + 1) * extra, :] = r_ref[s, half:]


def total_of(received, half):
    chips, tall, lanes = received.shape
    return pl.pallas_call(
        total_kernel,
        out_shape=(
            jax.ShapeDtypeStruct((half + chips * (tall - half), lanes), f32),
            jax.ShapeDtypeStruct((chips, half, lanes), f32),
        ),
        name="total",
    )(received)


def product_kernel(columns, at_ref, pcol_ref, a_ref, w_ref, g_ref, keep_ref, send_ref, r_ref):
    c, k = at_ref[0], at_ref[1]
    b = pl.program_id(0)
    rows, tn = a_ref.shape
    n = pcol_ref.shape[0]
    start = c * columns + b * tn
    onehot = onehot_rows(pcol_ref[...], start, tn)
    stays = (jnp.max(onehot, axis=0, keepdims=True) == 0) & (start + iota((1, tn), 1) >= n)
    hi, lo = split(jnp.where(stays, a_ref[...], 0.0), 2)
    w = w_ref[...]
    onehot = onehot.astype(bf16)
    r = folded(dot(w, jnp.concatenate([hi, onehot], axis=0))) + dot(w[:n, :rows], lo)
    r_ref[...] = r

    @pl.when((c == 0) & (b < n // tn))
    def _():
        r_ref[...] = g_ref[...]

    half = n // 2
    lanes = keep_ref.shape[2]
    for s in range(tn // lanes):
        cut = slice(s * lanes, (s + 1) * lanes)
        keep_ref[s] = r_ref[pl.ds(k * half, half), cut]
        send_ref[s] = r_ref[pl.ds((1 - k) * half, half), cut]


def product(at, pcol, a, w, g, chips):
    rows, columns = a.shape
    n = g.shape[0]
    tn = n
    lanes = columns // chips
    shape = (chips, n // 2, lanes)
    return pl.pallas_call(
        functools.partial(product_kernel, columns),
        out_shape=(jax.ShapeDtypeStruct(shape, f32),) * 2,
        grid_spec=pltpu.PrefetchScalarGridSpec(
            num_scalar_prefetch=1,
            grid=(columns // tn,),
            in_specs=[
                whole(pcol.shape),
                pl.BlockSpec((rows, tn), lambda b, *_: (0, b)),
                whole(w.shape),
                whole((n, n)),
            ],
            out_specs=(pl.BlockSpec((tn // lanes, n // 2, lanes), lambda b, *_: (b, 0, 0)),) * 2,
            scratch_shapes=[pltpu.VMEM((n, tn), f32)],
        ),
        name="product",
    )(at, pcol, a, w, g)


def permute_kernel(columns, at_ref, pcol_ref, a_ref, p_ref, d_ref, o_ref):
    c = at_ref[0]
    b = pl.program_id(0)
    tn = a_ref.shape[1]
    n = pcol_ref.shape[0]
    onehot = onehot_rows(pcol_ref[...], c * columns + b * tn, tn)
    here = jnp.max(onehot, axis=0, keepdims=True) > 0
    o_ref[...] = jnp.where(here, folded(dot(d_ref[...], onehot.astype(bf16))), a_ref[...])

    @pl.when((c == 0) & (b < n // tn))
    def _():
        o_ref[...] = p_ref[...]


def permute(at, pcol, a, p, d):
    rows, columns = a.shape
    n = p.shape[1]
    tn = n
    return pl.pallas_call(
        functools.partial(permute_kernel, columns),
        out_shape=jax.ShapeDtypeStruct(a.shape, f32),
        grid_spec=pltpu.PrefetchScalarGridSpec(
            num_scalar_prefetch=1,
            grid=(columns // tn,),
            in_specs=[
                whole(pcol.shape),
                pl.BlockSpec((rows, tn), lambda b, *_: (0, b)),
                whole((rows, n)),
                whole(d.shape),
            ],
            out_specs=pl.BlockSpec((rows, tn), lambda b, *_: (0, b)),
        ),
        name="permute",
    )(at, pcol, a, p, d)


def unit_inverse(block):
    nb = block.shape[0]
    wide = 2 * nb
    sub = 8
    eye = jnp.where(iota((nb, nb), 0) == iota((nb, nb), 1), 1.0, 0.0)
    full = jnp.concatenate([block, eye], axis=1)
    tiles = [full[i : i + sub] for i in range(0, nb, sub)]
    at = iota((sub, wide), 0)
    for i in range(len(tiles)):
        cols = [[jnp.broadcast_to(t[:, i * sub + q : i * sub + q + 1], (sub, wide)) for t in tiles[i:]] for q in range(sub)]
        for q in range(sub):
            pivot = cols[q][0][q : q + 1]
            rest = 1.0 / pivot
            mult = [m * rest for m in cols[q]]
            mult[0] = jnp.where(at > q, mult[0], 0.0)
            for later in cols[q + 1 :]:
                row = later[0][q : q + 1]
                for u, m in enumerate(mult):
                    later[u] = later[u] - m * row
            row = tiles[i][q : q + 1]
            for u, m in enumerate(mult):
                tiles[i + u] = tiles[i + u] - m * row
    done = jnp.concatenate(tiles, axis=0)
    diagonal = jnp.sum(jnp.where(iota((nb, wide), 0) == iota((nb, wide), 1), done, 0.0), axis=1, keepdims=True)
    return done[:, nb:] * lax.rsqrt(diagonal)


def factor_kernel(at_ref, mine_ref, other_ref, p_ref, inv_ref, il_ref, b_ref, t_ref):
    k = at_ref[1]
    n = p_ref.shape[1]
    lanes = mine_ref.shape[1]
    nb = 64
    half = n // 2
    width = n // lanes
    part = 8
    for s in range(half // part):
        for t in range(width):
            low = half + (s * width + t) * part
            cols = slice(t * lanes, (t + 1) * lanes)
            t_ref[pl.ds((2 * s + k) * part, part), cols] = mine_ref[low : low + part, :]
            t_ref[pl.ds((2 * s + 1 - k) * part, part), cols] = other_ref[low : low + part, :]
    t_ref[:, n:] = jnp.where(iota((n, n), 0) == iota((n, n), 1), 1.0, 0.0)
    for s in range(0, n, nb):
        inv = unit_inverse(t_ref[s : s + nb, s : s + nb])
        y = dot(inv, t_ref[s : s + nb, :], NN, highest)
        inv_ref[s : s + nb, :] = y[:, n:]
        if s + nb < n:
            t_ref[s + nb :, :] = t_ref[s + nb :, :] - dot(y[:, s + nb : n], y, TN, highest)
    inverse = inv_ref[...]
    il_ref[...] = stacked(inverse)
    b_ref[...] = stacked(dot(p_ref[...], inverse, NT, highest))


def factor(at, mine, other, p):
    rows, n = p.shape
    outs = (((n, n), f32), ((2 * n, n), bf16), ((2 * rows, n), bf16))
    return pl.pallas_call(
        factor_kernel,
        out_shape=tuple(jax.ShapeDtypeStruct(s, t) for s, t in outs),
        grid_spec=pltpu.PrefetchScalarGridSpec(
            num_scalar_prefetch=1,
            grid=(1,),
            in_specs=[whole(v.shape) for v in (mine, other, p)],
            out_specs=tuple(whole(s) for s, _ in outs),
            scratch_shapes=[pltpu.VMEM((n, 2 * n), f32)],
        ),
        name="factor",
    )(at, mine, other, p)


def share_kernel(columns, at_ref, prow_ref, mine_ref, other_ref, inv_ref, slots_ref, sk_ref, u_ref, o_ref, s_ref, t_ref):
    c, k, r = at_ref[0], at_ref[1], at_ref[2]
    n = inv_ref.shape[0]
    half = n // 2
    pieces, rows = sk_ref.shape
    s_ref[pl.ds(k * half, half), :] = mine_ref[:half]
    s_ref[pl.ds((1 - k) * half, half), :] = other_ref[:half]
    t_ref[...] = s_ref[...].T
    inverse = inv_ref[...]
    upper = dot(t_ref[pl.ds(k * pieces, pieces), :], inverse, NT, highest)
    u_ref[...] = upper
    solved = dot(upper, inverse, NN, highest)
    start = c * columns + r * pieces
    prow = prow_ref[...]
    place = start + iota((pieces, 1), 0)
    hit = jnp.where(place == prow, 1.0, 0.0)
    stays = (jnp.max(hit, axis=1, keepdims=True) == 0) & (place >= n)
    lead = jnp.where(place == iota((1, n), 1), 1.0, 0.0)
    old = sk_ref[...]
    slots = slots_ref[:rows]
    own = (prow >= start) & (prow < start + pieces)
    fronts = jnp.where(own, dot(old, hit, TN, highest), slots)
    back = dot(jnp.where(place >= n, hit, 0.0), slots, NT, highest)
    o_ref[...] = jnp.where(stays, old, 0.0) + back + dot(lead - solved, fronts, NT, highest)


def finish_share(at, prow, mine, other, inverse, slots, sketch, columns):
    n = inverse.shape[0]
    outs = ((sketch.shape[0], n), sketch.shape)
    return pl.pallas_call(
        functools.partial(share_kernel, columns),
        out_shape=tuple(jax.ShapeDtypeStruct(s, f32) for s in outs),
        grid_spec=pltpu.PrefetchScalarGridSpec(
            num_scalar_prefetch=1,
            grid=(1,),
            in_specs=[whole(v.shape) for v in (prow, mine, other, inverse, slots, sketch)],
            out_specs=tuple(whole(s) for s in outs),
            scratch_shapes=[pltpu.VMEM((n, mine.shape[1]), f32), pltpu.VMEM((mine.shape[1], n), f32)],
        ),
        name="share",
    )(at, prow, mine, other, inverse, slots, sketch)


def trailing_kernel(at_ref, a_ref, b_ref, inv_ref, mine_ref, other_ref, o_ref, s_ref):
    k = at_ref[1]
    parts, half, lanes = mine_ref.shape
    for s in range(parts):
        cut = slice(s * lanes, (s + 1) * lanes)
        s_ref[pl.ds(k * half, half), cut] = mine_ref[s]
        s_ref[pl.ds((1 - k) * half, half), cut] = other_ref[s]
    upper = product3(inv_ref[...], s_ref[...])
    o_ref[...] = a_ref[...] - product3(b_ref[...], upper)


def trail(at, a, b, inverse, mine, other):
    rows, columns = a.shape
    _, half, lanes = mine.shape
    n = 2 * half
    tn = n
    share = pl.BlockSpec((tn // lanes, half, lanes), lambda b, *_: (b, 0, 0))
    return pl.pallas_call(
        trailing_kernel,
        out_shape=jax.ShapeDtypeStruct(a.shape, f32),
        grid_spec=pltpu.PrefetchScalarGridSpec(
            num_scalar_prefetch=1,
            grid=(columns // tn,),
            in_specs=[pl.BlockSpec((rows, tn), lambda b, *_: (0, b)), whole(b.shape), whole(inverse.shape), share, share],
            out_specs=pl.BlockSpec((rows, tn), lambda b, *_: (0, b)),
            scratch_shapes=[pltpu.VMEM((n, tn), f32)],
        ),
        name="trailing",
    )(at, a, b, inverse, mine, other)


def exchange(pieces, axis):
    return lax.all_to_all(pieces, axis, split_axis=0, concat_axis=0, tiled=True)


def per_device(matrix, pivots, sketch):
    c = lax.axis_index("col")
    r = lax.axis_index(ROW)
    k = lax.axis_index("row_2")
    cols, lanes, chips = lax.axis_size("col"), lax.axis_size(ROW), lax.axis_size(CHIPS)
    rows, columns = matrix.shape
    n = pivots.shape[0]
    prow = pivots.reshape(1, n)
    at = scalars(c, k, r)
    swap = [(0, 1), (1, 0)]

    turned = sketch.T
    partner, pcol, part = prepare(at, prow, turned, columns, lanes)
    gathered = exchange(part, ROW)
    mine = extract(at, prow, partner, matrix)
    arrived = exchange(mine.reshape(cols, rows // cols, n), "col")
    line = gathered.sum(axis=0)
    inside = inside_of(at, prow, partner, matrix)
    message = holder(prow, arrived, line, columns)
    x = exchange(message, "col")
    panel, displaced, w, gram_part, message = gram(at, prow, x, mine, inside, line, columns, lanes)
    gram_pieces = exchange(message, ROW)
    keep, send = product(at, pcol, matrix, w, gram_part, chips)
    sent = lax.ppermute(send, "row_2", swap)
    half, slots = add_halves(keep, sent, gram_pieces, line.shape[0])
    summands = exchange(half, CHIPS)
    permuted = permute(at, pcol, matrix, panel, displaced)
    share, message = total_of(summands, n // 2)
    own_all = exchange(message, CHIPS)
    share_other = lax.ppermute(share, "row_2", swap)
    inverse, stack, basis = factor(at, share, share_other, panel)
    upper_share, new_sketch = finish_share(at, prow, share, share_other, inverse, slots, turned, columns)
    other_all = lax.ppermute(own_all, "row_2", swap)
    trailing = trail(at, permuted, basis, stack, own_all, other_all)
    return (upper_share.T, trailing, new_sketch.T)


def solution(mesh):
    finer = Mesh(mesh.devices.reshape(4, 4, 2, mesh.shape["col"]), ("row_0", "row_1", "row_2", "col"))
    return jax.shard_map(
        per_device,
        mesh=finer,
        in_specs=(P(ROW, "col"), P(), P(None, COL_ROW)),
        out_specs=(P(None, COL_ROW), P(ROW, "col"), P(None, COL_ROW)),
        check_vma=False,
    )
```

```python
import functools

import jax
import jax.numpy as jnp
from jax import lax
from jax.experimental import pallas as pl
from jax.experimental.pallas import tpu as pltpu
from jax.sharding import Mesh
from jax.sharding import PartitionSpec as P


ROW = ("row_0", "row_1", "row_2")
CHIPS = ("row_0", "row_1")
COL_ROW = ("col", "row_0", "row_1", "row_2")

f32, bf16, i32 = jnp.float32, jnp.bfloat16, jnp.int32
highest = lax.Precision.HIGHEST
NN = (((1,), (0,)), ((), ()))
NT = (((1,), (1,)), ((), ()))
TN = (((0,), (0,)), ((), ()))


def iota(shape, dim):
    return lax.broadcasted_iota(i32, shape, dim)


def dot(a, b, dims=NN, precision=None):
    return lax.dot_general(a, b, dims, precision=precision, preferred_element_type=f32)


def split(a, pieces):
    out = []
    for _ in range(pieces - 1):
        top = a.astype(bf16)
        out.append(top)
        a = a - top.astype(f32)
    return (*out, a.astype(bf16))


def stacked(a):
    return jnp.concatenate(split(a, 2), axis=0)


def folded(top_bottom):
    rows = top_bottom.shape[0] // 2
    return top_bottom[:rows] + top_bottom[rows:]


def product3(left, right):
    hi, lo = split(right, 2)
    return folded(dot(left, hi)) + dot(left[: left.shape[0] // 2], lo)


def abreast(a):
    return jnp.concatenate(split(a, 2), axis=1)


def twice(a):
    return jnp.concatenate([a, a], axis=0)


def owned(place, c, columns):
    return (place >= c * columns) & (place < (c + 1) * columns)


def onehot_rows(pcol, start, width):
    lanes = pcol.shape[1]
    return jnp.concatenate(
        [
            jnp.where(pcol[:, : min(lanes, width - s)] == start + s + iota((1, min(lanes, width - s)), 1), 1.0, 0.0)
            for s in range(0, width, lanes)
        ],
        axis=1,
    )


def in_vmem(value):
    return pltpu.with_memory_space_constraint(value, pltpu.VMEM)


def held():
    return pl.BlockSpec(memory_space=pltpu.VMEM)


def whole(shape):
    return pl.BlockSpec(shape, lambda *_: (0,) * len(shape))


def scalars(*values):
    return jnp.stack([jnp.asarray(v, i32) for v in values])


def columns_of(ref, buffer, sems, step):
    width = buffer.shape[2]
    cut = pl.ds(pl.multiple_of(step * width, width), width)
    return pltpu.make_async_copy(ref.at[:, cut], buffer.at[step], sems.at[step])


def columns_to(buffer, ref, sems, step):
    width = buffer.shape[2]
    cut = pl.ds(pl.multiple_of(step * width, width), width)
    return pltpu.make_async_copy(buffer.at[step], ref.at[:, cut], sems.at[step])


def each(count, body):
    def step(i, carry):
        body(i)
        return carry

    lax.fori_loop(0, count, step, 0)


def streams(shape, width):
    rows, columns = shape
    blocks = columns // width
    return [pltpu.VMEM((blocks, rows, width), f32), pltpu.SemaphoreType.DMA((blocks,))]


HBM = pl.BlockSpec(memory_space=pltpu.HBM)


def extract_kernel(at_ref, prow_ref, a_ref, m_ref, partner_ref, pcol_ref, a_buf, a_sem):
    n = prow_ref.shape[1]
    columns = a_ref.shape[1]
    blocks = a_buf.shape[0]
    c = at_ref[0]
    each(blocks, lambda b: columns_of(a_ref, a_buf, a_sem, b).start())
    prow = prow_ref[...]
    across = jnp.broadcast_to(prow.astype(f32), (n, n))
    down = across.T.astype(i32)
    pcol_ref[...] = down[:, : pcol_ref.shape[1]]
    named = jnp.where(iota((n, n), 0) == prow, 1.0, 0.0).astype(bf16)
    free = 1.0 - dot(named, jnp.ones((n, n), bf16))
    upto = jnp.where(iota((n, n), 1) <= iota((n, n), 0), 1.0, 0.0).astype(bf16)
    count = dot(upto, free.astype(bf16))
    rank = jnp.sum(jnp.where((down < prow) & (down >= n), 1.0, 0.0), axis=0, keepdims=True)
    partner = jnp.sum(jnp.where(count <= rank, 1.0, 0.0), axis=0, keepdims=True).astype(i32)
    partner = jnp.where(prow >= n, partner, -1)
    partner_ref[...] = partner
    sel = jnp.where(owned(prow, c, columns), prow - c * columns, jnp.where(c == 0, partner, -1))
    m_ref[...] = jnp.zeros(m_ref.shape, f32)

    def block(b):
        columns_of(a_ref, a_buf, a_sem, b).wait()
        onehot = jnp.where(iota((n, n), 0) == sel - b * n, 1.0, 0.0).astype(bf16)
        m_ref[...] += dot(abreast(a_buf[b]), twice(onehot))

    each(blocks, block)


def extract(at, prow, a):
    rows, _ = a.shape
    n = prow.shape[1]
    outs = (((rows, n), f32), ((1, n), i32), ((n, 128), i32))
    return pl.pallas_call(
        extract_kernel,
        out_shape=tuple(jax.ShapeDtypeStruct(s, t) for s, t in outs),
        grid_spec=pltpu.PrefetchScalarGridSpec(
            num_scalar_prefetch=1,
            grid=(1,),
            in_specs=[whole((1, n)), HBM],
            out_specs=tuple(whole(s) for s, _ in outs),
            scratch_shapes=streams(a.shape, n),
        ),
        name="extract",
    )(at, prow, a)


def pick_kernel(columns, at_ref, prow_ref, partner_ref, sk_ref, s_ref, i_ref):
    n = prow_ref.shape[1]
    c, r = at_ref[0], at_ref[2]
    prow = prow_ref[...]
    own = owned(prow, c, columns)
    partner = partner_ref[...]
    sel = jnp.where(own, prow - c * columns, jnp.where(c == 0, partner, -1))
    disp = jnp.where(own & (c == 0), partner, -1)
    pieces, rows = sk_ref.shape
    lanes, tall, _ = s_ref.shape
    size = -(-rows // lanes)
    place = r * pieces + iota((pieces, 1), 0)
    pick = jnp.concatenate([jnp.where(place == sel, 1.0, 0.0), jnp.where(place == disp, 1.0, 0.0)], axis=1)
    hi, lo = split(sk_ref[...], 2)
    pick = pick.astype(bf16)
    line = dot(hi, pick, TN) + dot(lo, pick, TN)
    for i in range(lanes):
        low, high = min(i * size, rows), min((i + 1) * size, rows)
        for ref, cols in ((s_ref, slice(0, n)), (i_ref, slice(n, 2 * n))):
            if high > low:
                ref[i, : high - low, :] = line[low:high, cols]
            ref[i, high - low :, :] = jnp.zeros((tall - (high - low), n), f32)


def pick_sketch(at, prow, partner, sketch, columns, lanes):
    n = prow.shape[1]
    size = padded_to(-(-sketch.shape[1] // lanes), 8)
    return pl.pallas_call(
        functools.partial(pick_kernel, columns),
        out_shape=(jax.ShapeDtypeStruct((lanes, size, n), f32),) * 2,
        grid_spec=pltpu.PrefetchScalarGridSpec(
            num_scalar_prefetch=1,
            grid=(1,),
            in_specs=[whole((1, n)), whole((1, n)), whole(sketch.shape)],
            out_specs=(whole((lanes, size, n)),) * 2,
        ),
        name="pick",
    )(at, prow, partner, sketch)


def inside_kernel(columns, at_ref, prow_ref, partner_ref, a_ref, d_ref):
    n = prow_ref.shape[1]
    c = at_ref[0]
    disp = jnp.where(owned(prow_ref[...], c, columns) & (c == 0), partner_ref[...], -1)
    d_ref[...] = folded(dot(stacked(a_ref[...]), jnp.where(iota((n, n), 0) == disp, 1.0, 0.0).astype(bf16)))


def inside_of(at, prow, partner, a):
    rows, columns = a.shape
    n = prow.shape[1]
    return pl.pallas_call(
        functools.partial(inside_kernel, columns),
        out_shape=jax.ShapeDtypeStruct((rows, n), f32),
        grid_spec=pltpu.PrefetchScalarGridSpec(
            num_scalar_prefetch=1,
            grid=(1,),
            in_specs=[whole((1, n)), whole((1, n)), whole((rows, n))],
            out_specs=whole((rows, n)),
        ),
        name="inside",
    )(at, prow, partner, a)


def padded_to(rows, multiple):
    return -(-rows // multiple) * multiple


def holder_kernel(columns, prow_ref, r_ref, line_ref, o_ref):
    peers, height, _ = r_ref.shape
    prow = prow_ref[...]
    panel = r_ref[0]
    for s in range(1, peers):
        panel = jnp.where(owned(prow, s, columns), r_ref[s], panel)
    for s in range(peers):
        o_ref[s, :height] = jnp.where(owned(prow, s, columns), r_ref[0], panel) if s else panel
        o_ref[s, height:] = line_ref[...]


def holder(prow, received, line, columns):
    peers, height, n = received.shape
    return pl.pallas_call(
        functools.partial(holder_kernel, columns),
        out_shape=jax.ShapeDtypeStruct((peers, height + line.shape[0], n), f32),
        in_specs=[held()] * 3,
        name="holder",
    )(prow, in_vmem(received), line)


def gram_kernel(columns, at_ref, prow_ref, x_ref, m_ref, d0_ref, line_ref, p_ref, d_ref, w_ref, g_ref, o_ref, x_s):
    c = at_ref[0]
    peers = x_ref.shape[0]
    rows, n = m_ref.shape
    height = rows // peers
    size = line_ref.shape[0]
    lanes = o_ref.shape[0]
    prow = prow_ref[...]
    own = owned(prow, c, columns)
    for s in range(peers):
        x_s[s * height : (s + 1) * height, :] = x_ref[s, :height]
    x = x_s[...]
    panel = jnp.where(own, m_ref[...], x)
    moved = jnp.where(c == 0, d0_ref[...], jnp.where(own, x, 0.0))
    p_ref[...] = panel
    d_ref[...] = abreast(moved)
    turned = panel.T
    total = dot(turned, panel, NN, highest)
    g_ref[...] = total
    left = stacked(turned)
    w_ref[:, :rows] = left
    w_ref[:, rows:] = stacked(product3(left, moved))
    got = [x_ref[s, height : height + size] for s in range(peers)]
    front = got[0]
    for s in range(1, peers):
        front = jnp.where(owned(prow, s, columns), got[s], front)
    back = jnp.where(c == 0, line_ref[...], got[0])
    part = n // lanes
    share = columns // lanes
    for i in range(lanes):
        o_ref[i, :part] = total[i * part : (i + 1) * part]
        o_ref[i, part:] = jnp.where(owned(prow, c * lanes + i, share), back, front)


def gram(at, prow, x, m, d0, line, columns, lanes):
    rows, n = m.shape
    piece = n // lanes + line.shape[0]
    outs = (
        ((rows, n), f32),
        ((rows, 2 * n), bf16),
        ((2 * n, rows + n), bf16),
        ((n, n), f32),
        ((lanes, piece, n), f32),
    )
    return pl.pallas_call(
        functools.partial(gram_kernel, columns),
        out_shape=tuple(jax.ShapeDtypeStruct(s, t) for s, t in outs),
        grid_spec=pltpu.PrefetchScalarGridSpec(
            num_scalar_prefetch=1,
            grid=(1,),
            in_specs=[held()] * 5,
            out_specs=tuple(whole(s) for s, _ in outs),
            scratch_shapes=[pltpu.VMEM((rows, n), f32)],
        ),
        name="gram",
    )(at, prow, in_vmem(x), m, d0, line)


def half_kernel(part, size, keep_ref, sent_ref, got_ref, o_ref, line_ref):
    chips, half, lanes = keep_ref.shape
    peers, _, n = got_ref.shape
    o_ref[:, :half, :] = keep_ref[...] + sent_ref[...]
    total = got_ref[0, :part]
    for s in range(1, peers):
        total = total + got_ref[s, :part]
    for s in range(chips):
        for t in range(n // lanes):
            o_ref[s, half + t * part : half + (t + 1) * part, :] = total[:, t * lanes : (t + 1) * lanes]

    for s in range(peers):
        line_ref[s * size : (s + 1) * size, :] = got_ref[s, part : part + size]


def add_halves(keep, sent, got, size):
    chips, half, lanes = keep.shape
    peers, _, n = got.shape
    part = n // peers
    tall = half + part * (n // lanes)
    return pl.pallas_call(
        functools.partial(half_kernel, part, size),
        out_shape=(
            jax.ShapeDtypeStruct((chips, tall, lanes), f32),
            jax.ShapeDtypeStruct((peers * size, n), f32),
        ),
        in_specs=[held()] * 3,
        name="half",
    )(keep, in_vmem(sent), in_vmem(got))


def total_kernel(r_ref, share_ref, o_ref):
    chips, half, _ = o_ref.shape
    extra = r_ref.shape[1] - half
    total = r_ref[0, :half]
    for s in range(1, chips):
        total = total + r_ref[s, :half]
    share_ref[:half, :] = total
    for s in range(chips):
        o_ref[s] = total
        share_ref[half + s * extra : half + (s + 1) * extra, :] = r_ref[s, half:]


def total_of(received, half):
    chips, tall, lanes = received.shape
    return pl.pallas_call(
        total_kernel,
        out_shape=(
            jax.ShapeDtypeStruct((half + chips * (tall - half), lanes), f32),
            jax.ShapeDtypeStruct((chips, half, lanes), f32),
        ),
        in_specs=[held()],
        name="total",
    )(in_vmem(received))


def product_kernel(at_ref, pcol_ref, a_ref, w_ref, g_ref, keep_ref, send_ref, r_ref, a_buf, a_sem, k_buf, k_sem, s_buf, s_sem):
    c, k = at_ref[0], at_ref[1]
    rows, columns = a_ref.shape
    blocks, _, tn = a_buf.shape
    n = pcol_ref.shape[0]
    half = n // 2
    lanes = keep_ref.shape[2]
    parts = tn // lanes
    each(blocks, lambda b: columns_of(a_ref, a_buf, a_sem, b).start())

    def out(buffer, ref, sems, b):
        return pltpu.make_async_copy(buffer.at[b], ref.at[pl.ds(b * parts, parts)], sems.at[b])

    def block(b):
        columns_of(a_ref, a_buf, a_sem, b).wait()
        start = c * columns + b * tn
        onehot = onehot_rows(pcol_ref[...], start, tn)
        stays = (jnp.max(onehot, axis=0, keepdims=True) == 0) & (start + iota((1, tn), 1) >= n)
        hi, lo = split(jnp.where(stays, a_buf[b], 0.0), 2)
        w = w_ref[...]
        onehot = onehot.astype(bf16)
        r_ref[...] = folded(dot(w, jnp.concatenate([hi, onehot], axis=0))) + dot(w[:n, :rows], lo)

        @pl.when((c == 0) & (b < n // tn))
        def _():
            r_ref[...] = g_ref[...]

        for s in range(parts):
            cut = slice(s * lanes, (s + 1) * lanes)
            k_buf[b, s] = r_ref[pl.ds(k * half, half), cut]
            s_buf[b, s] = r_ref[pl.ds((1 - k) * half, half), cut]
        out(k_buf, keep_ref, k_sem, b).start()
        out(s_buf, send_ref, s_sem, b).start()

    each(blocks, block)

    def finish(b):
        out(k_buf, keep_ref, k_sem, b).wait()
        out(s_buf, send_ref, s_sem, b).wait()

    each(blocks, finish)


def product(at, pcol, a, w, g, chips):
    _, columns = a.shape
    n = g.shape[0]
    lanes = columns // chips
    blocks = columns // n
    shape = (chips, n // 2, lanes)
    made = [pltpu.VMEM((blocks, chips // blocks, n // 2, lanes), f32), pltpu.SemaphoreType.DMA((blocks,))]
    return pl.pallas_call(
        product_kernel,
        out_shape=(jax.ShapeDtypeStruct(shape, f32),) * 2,
        grid_spec=pltpu.PrefetchScalarGridSpec(
            num_scalar_prefetch=1,
            grid=(1,),
            in_specs=[whole(pcol.shape), HBM, whole(w.shape), whole((n, n))],
            out_specs=(HBM,) * 2,
            scratch_shapes=[pltpu.VMEM((n, n), f32), *streams(a.shape, n), *made, *made],
        ),
        name="product",
    )(at, pcol, a, w, g)


def permute_kernel(at_ref, pcol_ref, a_ref, p_ref, d_ref, o_ref, a_buf, a_sem, o_buf, o_sem):
    c = at_ref[0]
    columns = a_ref.shape[1]
    blocks, _, tn = a_buf.shape
    n = pcol_ref.shape[0]
    each(blocks, lambda b: columns_of(a_ref, a_buf, a_sem, b).start())

    def block(b):
        columns_of(a_ref, a_buf, a_sem, b).wait()
        onehot = onehot_rows(pcol_ref[...], c * columns + b * tn, tn)
        here = jnp.max(onehot, axis=0, keepdims=True) > 0
        o_buf[b] = jnp.where(here, dot(d_ref[...], twice(onehot.astype(bf16))), a_buf[b])

        @pl.when((c == 0) & (b < n // tn))
        def _():
            o_buf[b] = p_ref[...]

        columns_to(o_buf, o_ref, o_sem, b).start()

    each(blocks, block)
    each(blocks, lambda b: columns_to(o_buf, o_ref, o_sem, b).wait())


def permute(at, pcol, a, p, d):
    rows, _ = a.shape
    n = p.shape[1]
    return pl.pallas_call(
        permute_kernel,
        out_shape=jax.ShapeDtypeStruct(a.shape, f32),
        grid_spec=pltpu.PrefetchScalarGridSpec(
            num_scalar_prefetch=1,
            grid=(1,),
            in_specs=[whole(pcol.shape), HBM, whole((rows, n)), whole(d.shape)],
            out_specs=HBM,
            scratch_shapes=[*streams(a.shape, n), *streams(a.shape, n)],
        ),
        name="permute",
    )(at, pcol, a, p, d)


def unit_inverse(block):
    nb = block.shape[0]
    wide = 2 * nb
    sub = 8
    eye = jnp.where(iota((nb, nb), 0) == iota((nb, nb), 1), 1.0, 0.0)
    full = jnp.concatenate([block, eye], axis=1)
    tiles = [full[i : i + sub] for i in range(0, nb, sub)]
    at = iota((sub, wide), 0)
    for i in range(len(tiles)):
        cols = [[jnp.broadcast_to(t[:, i * sub + q : i * sub + q + 1], (sub, wide)) for t in tiles[i:]] for q in range(sub)]
        for q in range(sub):
            pivot = cols[q][0][q : q + 1]
            rest = 1.0 / pivot
            mult = [m * rest for m in cols[q]]
            mult[0] = jnp.where(at > q, mult[0], 0.0)
            for later in cols[q + 1 :]:
                row = later[0][q : q + 1]
                for u, m in enumerate(mult):
                    later[u] = later[u] - m * row
            row = tiles[i][q : q + 1]
            for u, m in enumerate(mult):
                tiles[i + u] = tiles[i + u] - m * row
    done = jnp.concatenate(tiles, axis=0)
    diagonal = jnp.sum(jnp.where(iota((nb, wide), 0) == iota((nb, wide), 1), done, 0.0), axis=1, keepdims=True)
    return done[:, nb:] * lax.rsqrt(diagonal)


def factor_kernel(at_ref, mine_ref, other_ref, p_ref, inv_ref, b_ref, t_ref):
    k = at_ref[1]
    n = p_ref.shape[1]
    lanes = mine_ref.shape[1]
    nb = 64
    half = n // 2
    width = n // lanes
    part = 8
    for s in range(half // part):
        for t in range(width):
            low = half + (s * width + t) * part
            cols = slice(t * lanes, (t + 1) * lanes)
            t_ref[pl.ds((2 * s + k) * part, part), cols] = mine_ref[low : low + part, :]
            t_ref[pl.ds((2 * s + 1 - k) * part, part), cols] = other_ref[low : low + part, :]
    t_ref[:, n:] = jnp.where(iota((n, n), 0) == iota((n, n), 1), 1.0, 0.0)
    for s in range(0, n, nb):
        inv = unit_inverse(t_ref[s : s + nb, s : s + nb])
        y = dot(inv, t_ref[s : s + nb, :], NN, highest)
        inv_ref[s : s + nb, :] = y[:, n:]
        if s + nb < n:
            t_ref[s + nb :, :] = t_ref[s + nb :, :] - dot(y[:, s + nb : n], y, TN, highest)
    inverse = inv_ref[...]
    hi, lo = split(dot(p_ref[...], dot(inverse, inverse, TN, highest), NN, highest), 2)
    for s, part in enumerate((hi, hi, lo)):
        b_ref[:, s * n : (s + 1) * n] = part


def factor(at, mine, other, p):
    rows, n = p.shape
    outs = (((n, n), f32), ((rows, 3 * n), bf16))
    return pl.pallas_call(
        factor_kernel,
        out_shape=tuple(jax.ShapeDtypeStruct(s, t) for s, t in outs),
        grid_spec=pltpu.PrefetchScalarGridSpec(
            num_scalar_prefetch=1,
            grid=(1,),
            in_specs=[held()] * 3,
            out_specs=tuple(whole(s) for s, _ in outs),
            scratch_shapes=[pltpu.VMEM((n, 2 * n), f32)],
        ),
        name="factor",
    )(at, mine, in_vmem(other), p)


def sketch_kernel(columns, at_ref, prow_ref, slots_ref, sk_ref, f_ref, o_ref):
    n = prow_ref.shape[1]
    pieces, rows = sk_ref.shape
    start = at_ref[0] * columns + at_ref[2] * pieces
    prow = prow_ref[...]
    place = start + iota((pieces, 1), 0)
    hit = jnp.where(place == prow, 1.0, 0.0)
    stays = (jnp.max(hit, axis=1, keepdims=True) == 0) & (place >= n)
    old = sk_ref[...]
    slots = slots_ref[:rows]
    own = (prow >= start) & (prow < start + pieces)
    f_ref[...] = jnp.where(own, dot(old, hit, TN, highest), slots)
    o_ref[...] = jnp.where(stays, old, 0.0) + dot(jnp.where(place >= n, hit, 0.0), slots, NT, highest)


def swap_sketch(at, prow, slots, sketch, columns):
    n = prow.shape[1]
    outs = ((sketch.shape[1], n), sketch.shape)
    return pl.pallas_call(
        functools.partial(sketch_kernel, columns),
        out_shape=tuple(jax.ShapeDtypeStruct(s, f32) for s in outs),
        grid_spec=pltpu.PrefetchScalarGridSpec(
            num_scalar_prefetch=1,
            grid=(1,),
            in_specs=[whole(v.shape) for v in (prow, slots, sketch)],
            out_specs=tuple(whole(s) for s in outs),
        ),
        name="sketch",
    )(at, prow, slots, sketch)


def share_kernel(columns, at_ref, mine_ref, other_ref, inv_ref, fronts_ref, sk_ref, u_ref, o_ref, s_ref, t_ref):
    c, k, r = at_ref[0], at_ref[1], at_ref[2]
    n = inv_ref.shape[0]
    half = n // 2
    pieces, _ = sk_ref.shape
    s_ref[pl.ds(k * half, half), :] = mine_ref[:half]
    s_ref[pl.ds((1 - k) * half, half), :] = other_ref[:half]
    t_ref[...] = s_ref[...].T
    inverse = inv_ref[...]
    upper = dot(t_ref[pl.ds(k * pieces, pieces), :], inverse, NT, highest)
    u_ref[...] = upper
    solved = dot(upper, inverse, NN, highest)
    place = c * columns + r * pieces + iota((pieces, 1), 0)
    lead = jnp.where(place == iota((1, n), 1), 1.0, 0.0)
    o_ref[...] = sk_ref[...] + dot(lead - solved, fronts_ref[...], NT, highest)


def finish_share(at, mine, other, inverse, fronts, sketch, columns):
    n = inverse.shape[0]
    outs = ((sketch.shape[0], n), sketch.shape)
    return pl.pallas_call(
        functools.partial(share_kernel, columns),
        out_shape=tuple(jax.ShapeDtypeStruct(s, f32) for s in outs),
        grid_spec=pltpu.PrefetchScalarGridSpec(
            num_scalar_prefetch=1,
            grid=(1,),
            in_specs=[held()] * 5,
            out_specs=tuple(whole(s) for s in outs),
            scratch_shapes=[pltpu.VMEM((n, mine.shape[1]), f32), pltpu.VMEM((mine.shape[1], n), f32)],
        ),
        name="share",
    )(at, mine, in_vmem(other), inverse, in_vmem(fronts), in_vmem(sketch))


def trailing_kernel(at_ref, a_ref, b_ref, mine_ref, other_ref, o_ref, s_ref, a_buf, a_sem, o_buf, o_sem):
    k = at_ref[1]
    _, half, lanes = mine_ref.shape
    blocks, _, tn = a_buf.shape
    parts = tn // lanes
    each(blocks, lambda b: columns_of(a_ref, a_buf, a_sem, b).start())

    def block(b):
        for s in range(parts):
            cut = slice(s * lanes, (s + 1) * lanes)
            s_ref[pl.ds(k * half, half), cut] = mine_ref[b * parts + s]
            s_ref[pl.ds((1 - k) * half, half), cut] = other_ref[b * parts + s]
        hi, lo = split(s_ref[...], 2)
        columns_of(a_ref, a_buf, a_sem, b).wait()
        o_buf[b] = a_buf[b] - dot(b_ref[...], jnp.concatenate([hi, lo, hi], axis=0))
        columns_to(o_buf, o_ref, o_sem, b).start()

    each(blocks, block)
    each(blocks, lambda b: columns_to(o_buf, o_ref, o_sem, b).wait())


def trail(at, a, b, mine, other):
    n = 2 * mine.shape[1]
    return pl.pallas_call(
        trailing_kernel,
        out_shape=jax.ShapeDtypeStruct(a.shape, f32),
        grid_spec=pltpu.PrefetchScalarGridSpec(
            num_scalar_prefetch=1,
            grid=(1,),
            in_specs=[HBM, whole(b.shape), held(), held()],
            out_specs=HBM,
            scratch_shapes=[pltpu.VMEM((n, n), f32), *streams(a.shape, n), *streams(a.shape, n)],
        ),
        name="trailing",
    )(at, a, b, in_vmem(mine), in_vmem(other))


def exchange(pieces, axis):
    return lax.all_to_all(pieces, axis, split_axis=0, concat_axis=0, tiled=True)


def side_of(value, which, dim):
    return lax.dynamic_index_in_dim(value, which, dim, keepdims=False)


def halved(value, which, axis, swap, dim):
    size = value.shape[dim] // 2
    value = value.reshape(*value.shape[:dim], 2, size, *value.shape[dim + 1 :])
    return side_of(value, which, dim) + lax.ppermute(side_of(value, 1 - which, dim), axis, swap)


def sum_at_rows(value):
    y, x, k = (lax.axis_index(a) for a in ROW)
    value = value.reshape(4, 4, 2, *value.shape[1:])
    near, far = [(0, 1), (1, 0), (2, 3), (3, 2)], [(0, 3), (3, 0), (1, 2), (2, 1)]
    value = halved(value, k, "row_2", [(0, 1), (1, 0)], 2)[:, :, 0]
    value = halved(value, x >> 1, "row_1", far, 1)
    value = halved(value, x & 1, "row_1", near, 1)[:, 0]
    value = halved(value, y >> 1, "row_0", far, 0)
    return halved(value, y & 1, "row_0", near, 0)[0]


def per_device(matrix, pivots, sketch):
    c = lax.axis_index("col")
    r = lax.axis_index(ROW)
    k = lax.axis_index("row_2")
    cols, lanes, chips = lax.axis_size("col"), lax.axis_size(ROW), lax.axis_size(CHIPS)
    rows, columns = matrix.shape
    n = pivots.shape[0]
    prow = pivots.reshape(1, n)
    at = scalars(c, k, r)
    swap = [(0, 1), (1, 0)]

    turned = sketch.T
    mine, partner, pcol = extract(at, prow, matrix)
    arrived = exchange(mine.reshape(cols, rows // cols, n), "col")
    picks, insides = pick_sketch(at, prow, partner, turned, columns, lanes)
    line = sum_at_rows(picks)
    inside_line = sum_at_rows(insides)
    inside = inside_of(at, prow, partner, matrix)
    message = holder(prow, arrived, line, columns)
    x = exchange(message, "col")
    panel, displaced, w, gram_part, message = gram(at, prow, x, mine, inside, inside_line, columns, lanes)
    gram_pieces = exchange(message, ROW)
    keep, send = product(at, pcol, matrix, w, gram_part, chips)
    sent = lax.ppermute(send, "row_2", swap)
    half, slots = add_halves(keep, sent, gram_pieces, -(-sketch.shape[0] // lanes))
    summands = exchange(half, CHIPS)
    permuted = permute(at, pcol, matrix, panel, displaced)
    fronts, swapped = swap_sketch(at, prow, slots, turned, columns)
    share, message = total_of(summands, n // 2)
    own_all = exchange(message, CHIPS)
    share_other = lax.ppermute(share, "row_2", swap)
    inverse, basis = factor(at, share, share_other, panel)
    upper_share, new_sketch = finish_share(at, share, share_other, inverse, fronts, swapped, columns)
    other_all = lax.ppermute(own_all, "row_2", swap)
    trailing = trail(at, permuted, basis, own_all, other_all)
    return (upper_share.T, trailing, new_sketch.T)


def solution(mesh):
    finer = Mesh(mesh.devices.reshape(4, 4, 2, mesh.shape["col"]), ("row_0", "row_1", "row_2", "col"))
    return jax.shard_map(
        per_device,
        mesh=finer,
        in_specs=(P(ROW, "col"), P(), P(None, COL_ROW)),
        out_specs=(P(None, COL_ROW), P(ROW, "col"), P(None, COL_ROW)),
        check_vma=False,
    )
```

```python
import functools

import jax
import jax.numpy as jnp
from jax import lax
from jax.experimental import pallas as pl
from jax.experimental.pallas import tpu as pltpu
from jax.sharding import Mesh
from jax.sharding import PartitionSpec as P


ROW = ("row_0", "row_1", "row_2")
CHIPS = ("row_0", "row_1")
COL_ROW = ("col", "row_0", "row_1", "row_2")

f32, bf16, i32 = jnp.float32, jnp.bfloat16, jnp.int32
highest = lax.Precision.HIGHEST
NN = (((1,), (0,)), ((), ()))
NT = (((1,), (1,)), ((), ()))
TN = (((0,), (0,)), ((), ()))


def iota(shape, dim):
    return lax.broadcasted_iota(i32, shape, dim)


def dot(a, b, dims=NN, precision=None):
    return lax.dot_general(a, b, dims, precision=precision, preferred_element_type=f32)


def split(a, pieces):
    out = []
    for _ in range(pieces - 1):
        top = a.astype(bf16)
        out.append(top)
        a = a - top.astype(f32)
    return (*out, a.astype(bf16))


def stacked(a):
    return jnp.concatenate(split(a, 2), axis=0)


def folded(top_bottom):
    rows = top_bottom.shape[0] // 2
    return top_bottom[:rows] + top_bottom[rows:]


def product3(left, right):
    hi, lo = split(right, 2)
    return folded(dot(left, hi)) + dot(left[: left.shape[0] // 2], lo)


def abreast(a):
    return jnp.concatenate(split(a, 2), axis=1)


def twice(a):
    return jnp.concatenate([a, a], axis=0)


def owned(place, c, columns):
    return (place >= c * columns) & (place < (c + 1) * columns)


def onehot_rows(pcol, start, width):
    lanes = pcol.shape[1]
    return jnp.concatenate(
        [
            jnp.where(pcol[:, : min(lanes, width - s)] == start + s + iota((1, min(lanes, width - s)), 1), 1.0, 0.0)
            for s in range(0, width, lanes)
        ],
        axis=1,
    )


def in_vmem(value):
    return pltpu.with_memory_space_constraint(value, pltpu.VMEM)


def held():
    return pl.BlockSpec(memory_space=pltpu.VMEM)


def whole(shape):
    return pl.BlockSpec(shape, lambda *_: (0,) * len(shape))


def scalars(*values):
    return jnp.stack([jnp.asarray(v, i32) for v in values])


def columns_of(ref, buffer, sems, step):
    width = buffer.shape[2]
    cut = pl.ds(pl.multiple_of(step * width, width), width)
    return pltpu.make_async_copy(ref.at[:, cut], buffer.at[step], sems.at[step])


def columns_to(buffer, ref, sems, step):
    width = buffer.shape[2]
    cut = pl.ds(pl.multiple_of(step * width, width), width)
    return pltpu.make_async_copy(buffer.at[step], ref.at[:, cut], sems.at[step])


def each(count, body):
    def step(i, carry):
        body(i)
        return carry

    lax.fori_loop(0, count, step, 0)


def streams(shape, width):
    rows, columns = shape
    blocks = columns // width
    return [pltpu.VMEM((blocks, rows, width), f32), pltpu.SemaphoreType.DMA((blocks,))]


HBM = pl.BlockSpec(memory_space=pltpu.HBM)


def extract_kernel(at_ref, prow_ref, a_ref, m_ref, partner_ref, pcol_ref, a_buf, a_sem):
    n = prow_ref.shape[1]
    columns = a_ref.shape[1]
    blocks = a_buf.shape[0]
    c = at_ref[0]
    each(blocks, lambda b: columns_of(a_ref, a_buf, a_sem, b).start())
    prow = prow_ref[...]
    across = jnp.broadcast_to(prow.astype(f32), (n, n))
    down = across.T.astype(i32)
    pcol_ref[...] = down[:, : pcol_ref.shape[1]]
    named = jnp.where(iota((n, n), 0) == prow, 1.0, 0.0).astype(bf16)
    free = 1.0 - dot(named, jnp.ones((n, n), bf16))
    upto = jnp.where(iota((n, n), 1) <= iota((n, n), 0), 1.0, 0.0).astype(bf16)
    count = dot(upto, free.astype(bf16))
    rank = jnp.sum(jnp.where((down < prow) & (down >= n), 1.0, 0.0), axis=0, keepdims=True)
    partner = jnp.sum(jnp.where(count <= rank, 1.0, 0.0), axis=0, keepdims=True).astype(i32)
    partner = jnp.where(prow >= n, partner, -1)
    partner_ref[...] = partner
    sel = jnp.where(owned(prow, c, columns), prow - c * columns, jnp.where(c == 0, partner, -1))
    m_ref[...] = jnp.zeros(m_ref.shape, f32)

    def block(b):
        columns_of(a_ref, a_buf, a_sem, b).wait()
        onehot = jnp.where(iota((n, n), 0) == sel - b * n, 1.0, 0.0).astype(bf16)
        m_ref[...] += dot(abreast(a_buf[b]), twice(onehot))

    each(blocks, block)


def extract(at, prow, a):
    rows, _ = a.shape
    n = prow.shape[1]
    outs = (((rows, n), f32), ((1, n), i32), ((n, 128), i32))
    return pl.pallas_call(
        extract_kernel,
        out_shape=tuple(jax.ShapeDtypeStruct(s, t) for s, t in outs),
        grid_spec=pltpu.PrefetchScalarGridSpec(
            num_scalar_prefetch=1,
            grid=(1,),
            in_specs=[whole((1, n)), HBM],
            out_specs=tuple(whole(s) for s, _ in outs),
            scratch_shapes=streams(a.shape, n),
        ),
        name="extract",
    )(at, prow, a)


def pick_kernel(columns, at_ref, prow_ref, partner_ref, sk_ref, first_ref, s_ref):
    n = prow_ref.shape[1]
    c, r = at_ref[0], at_ref[2]
    prow = prow_ref[...]
    partner = partner_ref[...]
    sel = jnp.where(owned(prow, c, columns), prow - c * columns, jnp.where(c == 0, partner, -1))
    disp = jnp.where(owned(prow, 0, columns) & (c == 1), partner, -1)
    pieces, rows = sk_ref.shape
    lanes, tall, _ = s_ref.shape
    body = 8
    place = r * pieces + iota((pieces, 1), 0)
    pick = jnp.concatenate([jnp.where(place == sel, 1.0, 0.0), jnp.where(place == disp, 1.0, 0.0)], axis=0).astype(bf16)
    hi, lo = split(jnp.concatenate([sk_ref[...], first_ref[...]], axis=0), 2)
    line = dot(hi, pick, TN) + dot(lo, pick, TN)
    left = rows - lanes * body
    for i in range(lanes):
        s_ref[i, :body, :] = line[i * body : (i + 1) * body]
        s_ref[i, body:, :] = jnp.zeros((tall - body, n), f32)
        if i < left:
            s_ref[i, body : body + 1, :] = line[lanes * body + i : lanes * body + i + 1]


def pick_sketch(at, prow, partner, sketch, first, columns, lanes):
    n = prow.shape[1]
    return pl.pallas_call(
        functools.partial(pick_kernel, columns),
        out_shape=jax.ShapeDtypeStruct((lanes, 16, n), f32),
        grid_spec=pltpu.PrefetchScalarGridSpec(
            num_scalar_prefetch=1,
            grid=(1,),
            in_specs=[whole((1, n)), whole((1, n)), whole(sketch.shape), whole(sketch.shape)],
            out_specs=whole((lanes, 16, n)),
        ),
        name="pick",
    )(at, prow, partner, sketch, first)


def inside_kernel(columns, at_ref, prow_ref, partner_ref, a_ref, d_ref):
    n = prow_ref.shape[1]
    c = at_ref[0]
    disp = jnp.where(owned(prow_ref[...], c, columns) & (c == 0), partner_ref[...], -1)
    d_ref[...] = folded(dot(stacked(a_ref[...]), jnp.where(iota((n, n), 0) == disp, 1.0, 0.0).astype(bf16)))


def inside_of(at, prow, partner, a):
    rows, columns = a.shape
    n = prow.shape[1]
    return pl.pallas_call(
        functools.partial(inside_kernel, columns),
        out_shape=jax.ShapeDtypeStruct((rows, n), f32),
        grid_spec=pltpu.PrefetchScalarGridSpec(
            num_scalar_prefetch=1,
            grid=(1,),
            in_specs=[whole((1, n)), whole((1, n)), whole((rows, n))],
            out_specs=whole((rows, n)),
        ),
        name="inside",
    )(at, prow, partner, a)


def holder_kernel(columns, prow_ref, r_ref, line_ref, o_ref):
    peers, height, _ = r_ref.shape
    prow = prow_ref[...]
    panel = r_ref[0]
    for s in range(1, peers):
        panel = jnp.where(owned(prow, s, columns), r_ref[s], panel)
    for s in range(peers):
        o_ref[s, :height] = jnp.where(owned(prow, s, columns), r_ref[0], panel) if s else panel
        o_ref[s, height:] = line_ref[...]


def holder(prow, received, line, columns):
    peers, height, n = received.shape
    return pl.pallas_call(
        functools.partial(holder_kernel, columns),
        out_shape=jax.ShapeDtypeStruct((peers, height + line.shape[0], n), f32),
        in_specs=[held()] * 3,
        name="holder",
    )(prow, in_vmem(received), line)


def gram_kernel(columns, at_ref, prow_ref, x_ref, m_ref, d0_ref, p_ref, d_ref, w_ref, g_ref, o_ref, x_s):
    c = at_ref[0]
    peers = x_ref.shape[0]
    rows, n = m_ref.shape
    height = rows // peers
    size = x_ref.shape[1] - height
    lanes = o_ref.shape[0]
    prow = prow_ref[...]
    own = owned(prow, c, columns)
    for s in range(peers):
        x_s[s * height : (s + 1) * height, :] = x_ref[s, :height]
    x = x_s[...]
    panel = jnp.where(own, m_ref[...], x)
    moved = jnp.where(c == 0, d0_ref[...], jnp.where(own, x, 0.0))
    p_ref[...] = panel
    d_ref[...] = abreast(moved)
    turned = panel.T
    total = dot(turned, panel, NN, highest)
    g_ref[...] = total
    left = stacked(turned)
    w_ref[:, :rows] = left
    w_ref[:, rows:] = stacked(product3(left, moved))
    got = [x_ref[s, height : height + size] for s in range(peers)]
    front = got[0]
    for s in range(1, peers):
        front = jnp.where(owned(prow, s, columns), got[s], front)
    back = jnp.where(c == 0, got[1], got[0])
    part = n // lanes
    share = columns // lanes
    for i in range(lanes):
        o_ref[i, :part] = total[i * part : (i + 1) * part]
        o_ref[i, part:] = jnp.where(owned(prow, c * lanes + i, share), back, front)


def gram(at, prow, x, m, d0, columns, lanes):
    rows, n = m.shape
    piece = n // lanes + x.shape[1] - rows // x.shape[0]
    outs = (
        ((rows, n), f32),
        ((rows, 2 * n), bf16),
        ((2 * n, rows + n), bf16),
        ((n, n), f32),
        ((lanes, piece, n), f32),
    )
    return pl.pallas_call(
        functools.partial(gram_kernel, columns),
        out_shape=tuple(jax.ShapeDtypeStruct(s, t) for s, t in outs),
        grid_spec=pltpu.PrefetchScalarGridSpec(
            num_scalar_prefetch=1,
            grid=(1,),
            in_specs=[held()] * 4,
            out_specs=tuple(whole(s) for s, _ in outs),
            scratch_shapes=[pltpu.VMEM((rows, n), f32)],
        ),
        name="gram",
    )(at, prow, in_vmem(x), m, d0)


def half_kernel(part, keep_ref, sent_ref, got_ref, o_ref, line_ref):
    chips, half, lanes = keep_ref.shape
    peers, _, n = got_ref.shape
    o_ref[:, :half, :] = keep_ref[...] + sent_ref[...]
    total = got_ref[0, :part]
    for s in range(1, peers):
        total = total + got_ref[s, :part]
    for s in range(chips):
        for t in range(n // lanes):
            o_ref[s, half + t * part : half + (t + 1) * part, :] = total[:, t * lanes : (t + 1) * lanes]

    for s in range(peers):
        line_ref[s * 8 : (s + 1) * 8, :] = got_ref[s, part : part + 8]
    for s in range(line_ref.shape[0] - 8 * peers):
        line_ref[8 * peers + s : 8 * peers + s + 1, :] = got_ref[s, part + 8 : part + 9]


def add_halves(keep, sent, got, rows):
    chips, half, lanes = keep.shape
    peers, _, n = got.shape
    part = n // peers
    tall = half + part * (n // lanes)
    return pl.pallas_call(
        functools.partial(half_kernel, part),
        out_shape=(
            jax.ShapeDtypeStruct((chips, tall, lanes), f32),
            jax.ShapeDtypeStruct((rows, n), f32),
        ),
        in_specs=[held()] * 3,
        name="half",
    )(keep, in_vmem(sent), in_vmem(got))


def total_kernel(r_ref, share_ref, o_ref):
    chips, half, _ = o_ref.shape
    extra = r_ref.shape[1] - half
    total = r_ref[0, :half]
    for s in range(1, chips):
        total = total + r_ref[s, :half]
    share_ref[:half, :] = total
    for s in range(chips):
        o_ref[s] = total
        share_ref[half + s * extra : half + (s + 1) * extra, :] = r_ref[s, half:]


def total_of(received, half):
    chips, tall, lanes = received.shape
    return pl.pallas_call(
        total_kernel,
        out_shape=(
            jax.ShapeDtypeStruct((half + chips * (tall - half), lanes), f32),
            jax.ShapeDtypeStruct((chips, half, lanes), f32),
        ),
        in_specs=[held()],
        name="total",
    )(in_vmem(received))


def product_kernel(at_ref, pcol_ref, a_ref, w_ref, g_ref, keep_ref, send_ref, r_ref, a_buf, a_sem, k_buf, k_sem, s_buf, s_sem):
    c, k = at_ref[0], at_ref[1]
    rows, columns = a_ref.shape
    blocks, _, tn = a_buf.shape
    n = pcol_ref.shape[0]
    half = n // 2
    lanes = keep_ref.shape[2]
    parts = tn // lanes
    each(blocks, lambda b: columns_of(a_ref, a_buf, a_sem, b).start())

    def out(buffer, ref, sems, b):
        return pltpu.make_async_copy(buffer.at[b], ref.at[pl.ds(b * parts, parts)], sems.at[b])

    def block(b):
        columns_of(a_ref, a_buf, a_sem, b).wait()
        start = c * columns + b * tn
        onehot = onehot_rows(pcol_ref[...], start, tn)
        stays = (jnp.max(onehot, axis=0, keepdims=True) == 0) & (start + iota((1, tn), 1) >= n)
        hi, lo = split(jnp.where(stays, a_buf[b], 0.0), 2)
        w = w_ref[...]
        onehot = onehot.astype(bf16)
        r_ref[...] = folded(dot(w, jnp.concatenate([hi, onehot], axis=0))) + dot(w[:n, :rows], lo)

        @pl.when((c == 0) & (b < n // tn))
        def _():
            r_ref[...] = g_ref[...]

        for s in range(parts):
            cut = slice(s * lanes, (s + 1) * lanes)
            k_buf[b, s] = r_ref[pl.ds(k * half, half), cut]
            s_buf[b, s] = r_ref[pl.ds((1 - k) * half, half), cut]
        out(k_buf, keep_ref, k_sem, b).start()
        out(s_buf, send_ref, s_sem, b).start()

    each(blocks, block)

    def finish(b):
        out(k_buf, keep_ref, k_sem, b).wait()
        out(s_buf, send_ref, s_sem, b).wait()

    each(blocks, finish)


def product(at, pcol, a, w, g, chips):
    _, columns = a.shape
    n = g.shape[0]
    lanes = columns // chips
    blocks = columns // n
    shape = (chips, n // 2, lanes)
    made = [pltpu.VMEM((blocks, chips // blocks, n // 2, lanes), f32), pltpu.SemaphoreType.DMA((blocks,))]
    return pl.pallas_call(
        product_kernel,
        out_shape=(jax.ShapeDtypeStruct(shape, f32),) * 2,
        grid_spec=pltpu.PrefetchScalarGridSpec(
            num_scalar_prefetch=1,
            grid=(1,),
            in_specs=[whole(pcol.shape), HBM, whole(w.shape), whole((n, n))],
            out_specs=(HBM,) * 2,
            scratch_shapes=[pltpu.VMEM((n, n), f32), *streams(a.shape, n), *made, *made],
        ),
        name="product",
    )(at, pcol, a, w, g)


def permute_kernel(at_ref, pcol_ref, a_ref, p_ref, d_ref, o_ref, a_buf, a_sem, o_buf, o_sem):
    c = at_ref[0]
    columns = a_ref.shape[1]
    blocks, _, tn = a_buf.shape
    n = pcol_ref.shape[0]
    each(blocks, lambda b: columns_of(a_ref, a_buf, a_sem, b).start())

    def block(b):
        columns_of(a_ref, a_buf, a_sem, b).wait()
        onehot = onehot_rows(pcol_ref[...], c * columns + b * tn, tn)
        here = jnp.max(onehot, axis=0, keepdims=True) > 0
        o_buf[b] = jnp.where(here, dot(d_ref[...], twice(onehot.astype(bf16))), a_buf[b])

        @pl.when((c == 0) & (b < n // tn))
        def _():
            o_buf[b] = p_ref[...]

        columns_to(o_buf, o_ref, o_sem, b).start()

    each(blocks, block)
    each(blocks, lambda b: columns_to(o_buf, o_ref, o_sem, b).wait())


def permute(at, pcol, a, p, d):
    rows, _ = a.shape
    n = p.shape[1]
    return pl.pallas_call(
        permute_kernel,
        out_shape=jax.ShapeDtypeStruct(a.shape, f32),
        grid_spec=pltpu.PrefetchScalarGridSpec(
            num_scalar_prefetch=1,
            grid=(1,),
            in_specs=[whole(pcol.shape), HBM, whole((rows, n)), whole(d.shape)],
            out_specs=HBM,
            scratch_shapes=[*streams(a.shape, n), *streams(a.shape, n)],
        ),
        name="permute",
    )(at, pcol, a, p, d)


def unit_inverse(block):
    nb = block.shape[0]
    wide = 2 * nb
    sub = 8
    eye = jnp.where(iota((nb, nb), 0) == iota((nb, nb), 1), 1.0, 0.0)
    full = jnp.concatenate([block, eye], axis=1)
    tiles = [full[i : i + sub] for i in range(0, nb, sub)]
    at = iota((sub, wide), 0)
    for i in range(len(tiles)):
        cols = [[jnp.broadcast_to(t[:, i * sub + q : i * sub + q + 1], (sub, wide)) for t in tiles[i:]] for q in range(sub)]
        for q in range(sub):
            pivot = cols[q][0][q : q + 1]
            rest = 1.0 / pivot
            mult = [m * rest for m in cols[q]]
            mult[0] = jnp.where(at > q, mult[0], 0.0)
            for later in cols[q + 1 :]:
                row = later[0][q : q + 1]
                for u, m in enumerate(mult):
                    later[u] = later[u] - m * row
            row = tiles[i][q : q + 1]
            for u, m in enumerate(mult):
                tiles[i + u] = tiles[i + u] - m * row
    done = jnp.concatenate(tiles, axis=0)
    diagonal = jnp.sum(jnp.where(iota((nb, wide), 0) == iota((nb, wide), 1), done, 0.0), axis=1, keepdims=True)
    return done[:, nb:] * lax.rsqrt(diagonal)


def factor_kernel(at_ref, mine_ref, other_ref, p_ref, inv_ref, b_ref, t_ref):
    k = at_ref[1]
    n = p_ref.shape[1]
    lanes = mine_ref.shape[1]
    nb = 64
    half = n // 2
    width = n // lanes
    part = 8
    for s in range(half // part):
        for t in range(width):
            low = half + (s * width + t) * part
            cols = slice(t * lanes, (t + 1) * lanes)
            t_ref[pl.ds((2 * s + k) * part, part), cols] = mine_ref[low : low + part, :]
            t_ref[pl.ds((2 * s + 1 - k) * part, part), cols] = other_ref[low : low + part, :]
    t_ref[:, n:] = jnp.where(iota((n, n), 0) == iota((n, n), 1), 1.0, 0.0)
    for s in range(0, n, nb):
        inv = unit_inverse(t_ref[s : s + nb, s : s + nb])
        y = dot(inv, t_ref[s : s + nb, :], NN, highest)
        inv_ref[s : s + nb, :] = y[:, n:]
        if s + nb < n:
            t_ref[s + nb :, :] = t_ref[s + nb :, :] - dot(y[:, s + nb : n], y, TN, highest)
    inverse = inv_ref[...]
    hi, lo = split(dot(p_ref[...], dot(inverse, inverse, TN, highest), NN, highest), 2)
    for s, part in enumerate((hi, hi, lo)):
        b_ref[:, s * n : (s + 1) * n] = part


def factor(at, mine, other, p):
    rows, n = p.shape
    outs = (((n, n), f32), ((rows, 3 * n), bf16))
    return pl.pallas_call(
        factor_kernel,
        out_shape=tuple(jax.ShapeDtypeStruct(s, t) for s, t in outs),
        grid_spec=pltpu.PrefetchScalarGridSpec(
            num_scalar_prefetch=1,
            grid=(1,),
            in_specs=[held()] * 3,
            out_specs=tuple(whole(s) for s, _ in outs),
            scratch_shapes=[pltpu.VMEM((n, 2 * n), f32)],
        ),
        name="factor",
    )(at, mine, in_vmem(other), p)


def sketch_kernel(columns, at_ref, prow_ref, slots_ref, sk_ref, f_ref, o_ref):
    n = prow_ref.shape[1]
    pieces, _ = sk_ref.shape
    start = at_ref[0] * columns + at_ref[2] * pieces
    prow = prow_ref[...]
    place = start + iota((pieces, 1), 0)
    hit = jnp.where(place == prow, 1.0, 0.0)
    stays = (jnp.max(hit, axis=1, keepdims=True) == 0) & (place >= n)
    old = sk_ref[...]
    slots = slots_ref[...]
    own = (prow >= start) & (prow < start + pieces)
    f_ref[...] = jnp.where(own, dot(old, hit, TN, highest), slots)
    o_ref[...] = jnp.where(stays, old, 0.0) + dot(jnp.where(place >= n, hit, 0.0), slots, NT, highest)


def swap_sketch(at, prow, slots, sketch, columns):
    n = prow.shape[1]
    outs = ((sketch.shape[1], n), sketch.shape)
    return pl.pallas_call(
        functools.partial(sketch_kernel, columns),
        out_shape=tuple(jax.ShapeDtypeStruct(s, f32) for s in outs),
        grid_spec=pltpu.PrefetchScalarGridSpec(
            num_scalar_prefetch=1,
            grid=(1,),
            in_specs=[whole(v.shape) for v in (prow, slots, sketch)],
            out_specs=tuple(whole(s) for s in outs),
        ),
        name="sketch",
    )(at, prow, slots, sketch)


def share_kernel(columns, at_ref, mine_ref, other_ref, inv_ref, fronts_ref, sk_ref, u_ref, o_ref, s_ref, t_ref):
    c, k, r = at_ref[0], at_ref[1], at_ref[2]
    n = inv_ref.shape[0]
    half = n // 2
    pieces, _ = sk_ref.shape
    s_ref[pl.ds(k * half, half), :] = mine_ref[:half]
    s_ref[pl.ds((1 - k) * half, half), :] = other_ref[:half]
    t_ref[...] = s_ref[...].T
    inverse = inv_ref[...]
    upper = dot(t_ref[pl.ds(k * pieces, pieces), :], inverse, NT, highest)
    u_ref[...] = upper
    solved = dot(upper, inverse, NN, highest)
    place = c * columns + r * pieces + iota((pieces, 1), 0)
    lead = jnp.where(place == iota((1, n), 1), 1.0, 0.0)
    o_ref[...] = sk_ref[...] + dot(lead - solved, fronts_ref[...], NT, highest)


def finish_share(at, mine, other, inverse, fronts, sketch, columns):
    n = inverse.shape[0]
    outs = ((sketch.shape[0], n), sketch.shape)
    return pl.pallas_call(
        functools.partial(share_kernel, columns),
        out_shape=tuple(jax.ShapeDtypeStruct(s, f32) for s in outs),
        grid_spec=pltpu.PrefetchScalarGridSpec(
            num_scalar_prefetch=1,
            grid=(1,),
            in_specs=[held()] * 5,
            out_specs=tuple(whole(s) for s in outs),
            scratch_shapes=[pltpu.VMEM((n, mine.shape[1]), f32), pltpu.VMEM((mine.shape[1], n), f32)],
        ),
        name="share",
    )(at, mine, in_vmem(other), inverse, in_vmem(fronts), in_vmem(sketch))


def trailing_kernel(at_ref, a_ref, b_ref, mine_ref, other_ref, o_ref, s_ref, a_buf, a_sem, o_buf, o_sem):
    k = at_ref[1]
    _, half, lanes = mine_ref.shape
    blocks, _, tn = a_buf.shape
    parts = tn // lanes
    each(blocks, lambda b: columns_of(a_ref, a_buf, a_sem, b).start())

    def block(b):
        for s in range(parts):
            cut = slice(s * lanes, (s + 1) * lanes)
            s_ref[pl.ds(k * half, half), cut] = mine_ref[b * parts + s]
            s_ref[pl.ds((1 - k) * half, half), cut] = other_ref[b * parts + s]
        hi, lo = split(s_ref[...], 2)
        columns_of(a_ref, a_buf, a_sem, b).wait()
        o_buf[b] = a_buf[b] - dot(b_ref[...], jnp.concatenate([hi, lo, hi], axis=0))
        columns_to(o_buf, o_ref, o_sem, b).start()

    each(blocks, block)
    each(blocks, lambda b: columns_to(o_buf, o_ref, o_sem, b).wait())


def trail(at, a, b, mine, other):
    n = 2 * mine.shape[1]
    return pl.pallas_call(
        trailing_kernel,
        out_shape=jax.ShapeDtypeStruct(a.shape, f32),
        grid_spec=pltpu.PrefetchScalarGridSpec(
            num_scalar_prefetch=1,
            grid=(1,),
            in_specs=[HBM, whole(b.shape), held(), held()],
            out_specs=HBM,
            scratch_shapes=[pltpu.VMEM((n, n), f32), *streams(a.shape, n), *streams(a.shape, n)],
        ),
        name="trailing",
    )(at, a, b, in_vmem(mine), in_vmem(other))


def exchange(pieces, axis):
    return lax.all_to_all(pieces, axis, split_axis=0, concat_axis=0, tiled=True)


def side_of(value, which, dim):
    return lax.dynamic_index_in_dim(value, which, dim, keepdims=False)


def halved(value, which, axis, swap, dim):
    size = value.shape[dim] // 2
    value = value.reshape(*value.shape[:dim], 2, size, *value.shape[dim + 1 :])
    return side_of(value, which, dim) + lax.ppermute(side_of(value, 1 - which, dim), axis, swap)


def sum_at_rows(value):
    y, x, k = (lax.axis_index(a) for a in ROW)
    value = value.reshape(4, 4, 2, *value.shape[1:])
    near, far = [(0, 1), (1, 0), (2, 3), (3, 2)], [(0, 3), (3, 0), (1, 2), (2, 1)]
    value = halved(value, k, "row_2", [(0, 1), (1, 0)], 2)[:, :, 0]
    value = halved(value, x >> 1, "row_1", far, 1)
    value = halved(value, x & 1, "row_1", near, 1)[:, 0]
    value = halved(value, y >> 1, "row_0", far, 0)
    return halved(value, y & 1, "row_0", near, 0)[0]


def per_device(matrix, pivots, sketch):
    c = lax.axis_index("col")
    r = lax.axis_index(ROW)
    k = lax.axis_index("row_2")
    cols, lanes, chips = lax.axis_size("col"), lax.axis_size(ROW), lax.axis_size(CHIPS)
    rows, columns = matrix.shape
    n = pivots.shape[0]
    prow = pivots.reshape(1, n)
    at = scalars(c, k, r)
    swap = [(0, 1), (1, 0)]

    turned = sketch.T
    first = lax.ppermute(turned, "col", [(i, (i + 1) % cols) for i in range(cols)])
    mine, partner, pcol = extract(at, prow, matrix)
    arrived = exchange(mine.reshape(cols, rows // cols, n), "col")
    picks = pick_sketch(at, prow, partner, turned, first, columns, lanes)
    line = sum_at_rows(picks)
    inside = inside_of(at, prow, partner, matrix)
    message = holder(prow, arrived, line, columns)
    x = exchange(message, "col")
    panel, displaced, w, gram_part, message = gram(at, prow, x, mine, inside, columns, lanes)
    gram_pieces = exchange(message, ROW)
    keep, send = product(at, pcol, matrix, w, gram_part, chips)
    sent = lax.ppermute(send, "row_2", swap)
    half, slots = add_halves(keep, sent, gram_pieces, sketch.shape[0])
    summands = exchange(half, CHIPS)
    permuted = permute(at, pcol, matrix, panel, displaced)
    fronts, swapped = swap_sketch(at, prow, slots, turned, columns)
    share, message = total_of(summands, n // 2)
    own_all = exchange(message, CHIPS)
    share_other = lax.ppermute(share, "row_2", swap)
    inverse, basis = factor(at, share, share_other, panel)
    upper_share, new_sketch = finish_share(at, share, share_other, inverse, fronts, swapped, columns)
    other_all = lax.ppermute(own_all, "row_2", swap)
    trailing = trail(at, permuted, basis, own_all, other_all)
    return (upper_share.T, trailing, new_sketch.T)


def solution(mesh):
    finer = Mesh(mesh.devices.reshape(4, 4, 2, mesh.shape["col"]), ("row_0", "row_1", "row_2", "col"))
    return jax.shard_map(
        per_device,
        mesh=finer,
        in_specs=(P(ROW, "col"), P(), P(None, COL_ROW)),
        out_specs=(P(None, COL_ROW), P(ROW, "col"), P(None, COL_ROW)),
        check_vma=False,
    )
```

```python
import functools

import jax
import jax.numpy as jnp
from jax import lax
from jax.experimental import pallas as pl
from jax.experimental.pallas import tpu as pltpu
from jax.sharding import Mesh
from jax.sharding import PartitionSpec as P


ROW = ("row_0", "row_1", "row_2")
CHIPS = ("row_0", "row_1")
COL_ROW = ("col", "row_0", "row_1", "row_2")

f32, bf16, i32 = jnp.float32, jnp.bfloat16, jnp.int32
highest = lax.Precision.HIGHEST
NN = (((1,), (0,)), ((), ()))
NT = (((1,), (1,)), ((), ()))
TN = (((0,), (0,)), ((), ()))


def iota(shape, dim):
    return lax.broadcasted_iota(i32, shape, dim)


def dot(a, b, dims=NN, precision=None):
    return lax.dot_general(a, b, dims, precision=precision, preferred_element_type=f32)


def split(a, pieces):
    out = []
    for _ in range(pieces - 1):
        top = a.astype(bf16)
        out.append(top)
        a = a - top.astype(f32)
    return (*out, a.astype(bf16))


def stacked(a):
    return jnp.concatenate(split(a, 2), axis=0)


def folded(top_bottom):
    rows = top_bottom.shape[0] // 2
    return top_bottom[:rows] + top_bottom[rows:]


def product3(left, right):
    hi, lo = split(right, 2)
    return folded(dot(left, hi)) + dot(left[: left.shape[0] // 2], lo)


def abreast(a):
    return jnp.concatenate(split(a, 2), axis=1)


def twice(a):
    return jnp.concatenate([a, a], axis=0)


def owned(place, c, columns):
    return (place >= c * columns) & (place < (c + 1) * columns)


def onehot_rows(pcol, start, width):
    lanes = pcol.shape[1]
    return jnp.concatenate(
        [
            jnp.where(pcol[:, : min(lanes, width - s)] == start + s + iota((1, min(lanes, width - s)), 1), 1.0, 0.0)
            for s in range(0, width, lanes)
        ],
        axis=1,
    )


def in_vmem(value):
    return pltpu.with_memory_space_constraint(value, pltpu.VMEM)


def held():
    return pl.BlockSpec(memory_space=pltpu.VMEM)


def whole(shape):
    return pl.BlockSpec(shape, lambda *_: (0,) * len(shape))


def scalars(*values):
    return jnp.stack([jnp.asarray(v, i32) for v in values])


def columns_of(ref, buffer, sems, step):
    width = buffer.shape[2]
    cut = pl.ds(pl.multiple_of(step * width, width), width)
    return pltpu.make_async_copy(ref.at[:, cut], buffer.at[step], sems.at[step])


def columns_to(buffer, ref, sems, step):
    width = buffer.shape[2]
    cut = pl.ds(pl.multiple_of(step * width, width), width)
    return pltpu.make_async_copy(buffer.at[step], ref.at[:, cut], sems.at[step])


def each(count, body):
    def step(i, carry):
        body(i)
        return carry

    lax.fori_loop(0, count, step, 0)


def streams(shape, width):
    rows, columns = shape
    blocks = columns // width
    return [pltpu.VMEM((blocks, rows, width), f32), pltpu.SemaphoreType.DMA((blocks,))]


HBM = pl.BlockSpec(memory_space=pltpu.HBM)


def extract_kernel(at_ref, prow_ref, a_ref, m_ref, partner_ref, pcol_ref, a_buf, a_sem):
    n = prow_ref.shape[1]
    columns = a_ref.shape[1]
    blocks = a_buf.shape[0]
    c = at_ref[0]
    each(blocks, lambda b: columns_of(a_ref, a_buf, a_sem, b).start())
    prow = prow_ref[...]
    across = jnp.broadcast_to(prow.astype(f32), (n, n))
    down = across.T.astype(i32)
    pcol_ref[...] = down[:, : pcol_ref.shape[1]]
    named = jnp.where(iota((n, n), 0) == prow, 1.0, 0.0).astype(bf16)
    free = 1.0 - dot(named, jnp.ones((n, n), bf16))
    upto = jnp.where(iota((n, n), 1) <= iota((n, n), 0), 1.0, 0.0).astype(bf16)
    count = dot(upto, free.astype(bf16))
    rank = jnp.sum(jnp.where((down < prow) & (down >= n), 1.0, 0.0), axis=0, keepdims=True)
    partner = jnp.sum(jnp.where(count <= rank, 1.0, 0.0), axis=0, keepdims=True).astype(i32)
    partner = jnp.where(prow >= n, partner, -1)
    partner_ref[...] = partner
    sel = jnp.where(owned(prow, c, columns), prow - c * columns, jnp.where(c == 0, partner, -1))
    m_ref[...] = jnp.zeros(m_ref.shape, f32)

    def block(b):
        columns_of(a_ref, a_buf, a_sem, b).wait()
        onehot = jnp.where(iota((n, n), 0) == sel - b * n, 1.0, 0.0).astype(bf16)
        m_ref[...] += dot(abreast(a_buf[b]), twice(onehot))

    each(blocks, block)


def extract(at, prow, a):
    rows, _ = a.shape
    n = prow.shape[1]
    outs = (((rows, n), f32), ((1, n), i32), ((n, 128), i32))
    return pl.pallas_call(
        extract_kernel,
        out_shape=tuple(jax.ShapeDtypeStruct(s, t) for s, t in outs),
        grid_spec=pltpu.PrefetchScalarGridSpec(
            num_scalar_prefetch=1,
            grid=(1,),
            in_specs=[whole((1, n)), HBM],
            out_specs=tuple(whole(s) for s, _ in outs),
            scratch_shapes=streams(a.shape, n),
        ),
        name="extract",
    )(at, prow, a)


def pick_kernel(columns, at_ref, prow_ref, partner_ref, sk_ref, first_ref, s_ref):
    n = prow_ref.shape[1]
    c, r = at_ref[0], at_ref[2]
    prow = prow_ref[...]
    partner = partner_ref[...]
    sel = jnp.where(owned(prow, c, columns), prow - c * columns, jnp.where(c == 0, partner, -1))
    disp = jnp.where(owned(prow, 0, columns) & (c == 1), partner, -1)
    pieces, rows = sk_ref.shape
    lanes, tall, _ = s_ref.shape
    body = 8
    place = r * pieces + iota((pieces, 1), 0)
    pick = jnp.concatenate([jnp.where(place == sel, 1.0, 0.0), jnp.where(place == disp, 1.0, 0.0)], axis=0).astype(bf16)
    hi, lo = split(jnp.concatenate([sk_ref[...], first_ref[...]], axis=0), 2)
    line = dot(hi, pick, TN) + dot(lo, pick, TN)
    left = rows - lanes * body
    for i in range(lanes):
        s_ref[i, :body, :] = line[i * body : (i + 1) * body]
        s_ref[i, body:, :] = jnp.zeros((tall - body, n), f32)
        if i < left:
            s_ref[i, body : body + 1, :] = line[lanes * body + i : lanes * body + i + 1]


def pick_sketch(at, prow, partner, sketch, first, columns, lanes):
    n = prow.shape[1]
    return pl.pallas_call(
        functools.partial(pick_kernel, columns),
        out_shape=jax.ShapeDtypeStruct((lanes, 16, n), f32),
        grid_spec=pltpu.PrefetchScalarGridSpec(
            num_scalar_prefetch=1,
            grid=(1,),
            in_specs=[whole((1, n)), whole((1, n)), whole(sketch.shape), whole(sketch.shape)],
            out_specs=whole((lanes, 16, n)),
        ),
        name="pick",
    )(at, prow, partner, sketch, first)


def inside_kernel(columns, at_ref, prow_ref, partner_ref, a_ref, d_ref):
    n = prow_ref.shape[1]
    c = at_ref[0]
    disp = jnp.where(owned(prow_ref[...], c, columns) & (c == 0), partner_ref[...], -1)
    d_ref[...] = folded(dot(stacked(a_ref[...]), jnp.where(iota((n, n), 0) == disp, 1.0, 0.0).astype(bf16)))


def inside_of(at, prow, partner, a):
    rows, columns = a.shape
    n = prow.shape[1]
    return pl.pallas_call(
        functools.partial(inside_kernel, columns),
        out_shape=jax.ShapeDtypeStruct((rows, n), f32),
        grid_spec=pltpu.PrefetchScalarGridSpec(
            num_scalar_prefetch=1,
            grid=(1,),
            in_specs=[whole((1, n)), whole((1, n)), whole((rows, n))],
            out_specs=whole((rows, n)),
        ),
        name="inside",
    )(at, prow, partner, a)


def holder_kernel(columns, prow_ref, r_ref, o_ref):
    peers, _, _ = r_ref.shape
    prow = prow_ref[...]
    panel = r_ref[0]
    for s in range(1, peers):
        panel = jnp.where(owned(prow, s, columns), r_ref[s], panel)
    for s in range(peers):
        o_ref[s] = jnp.where(owned(prow, s, columns), r_ref[0], panel) if s else panel


def holder(prow, received, columns):
    return pl.pallas_call(
        functools.partial(holder_kernel, columns),
        out_shape=jax.ShapeDtypeStruct(received.shape, f32),
        in_specs=[held()] * 2,
        name="holder",
    )(prow, in_vmem(received))


def gram_kernel(columns, at_ref, prow_ref, x_ref, m_ref, d0_ref, p_ref, d_ref, w_ref, g_ref):
    c = at_ref[0]
    rows, _ = m_ref.shape
    prow = prow_ref[...]
    own = owned(prow, c, columns)
    x = x_ref[...]
    panel = jnp.where(own, m_ref[...], x)
    moved = jnp.where(c == 0, d0_ref[...], jnp.where(own, x, 0.0))
    p_ref[...] = panel
    d_ref[...] = abreast(moved)
    turned = panel.T
    g_ref[...] = dot(turned, panel, NN, highest)
    left = stacked(turned)
    w_ref[:, :rows] = left
    w_ref[:, rows:] = stacked(product3(left, moved))


def gram(at, prow, x, m, d0, columns):
    rows, n = m.shape
    outs = (((rows, n), f32), ((rows, 2 * n), bf16), ((2 * n, rows + n), bf16), ((n, n), f32))
    return pl.pallas_call(
        functools.partial(gram_kernel, columns),
        out_shape=tuple(jax.ShapeDtypeStruct(s, t) for s, t in outs),
        grid_spec=pltpu.PrefetchScalarGridSpec(
            num_scalar_prefetch=1,
            grid=(1,),
            in_specs=[held()] * 4,
            out_specs=tuple(whole(s) for s, _ in outs),
        ),
        name="gram",
    )(at, prow, in_vmem(x), m, d0)


def message_kernel(columns, at_ref, prow_ref, g_ref, got_ref, o_ref):
    c = at_ref[0]
    peers = got_ref.shape[0]
    lanes = o_ref.shape[0]
    n = g_ref.shape[0]
    prow = prow_ref[...]
    front = got_ref[0]
    for s in range(1, peers):
        front = jnp.where(owned(prow, s, columns), got_ref[s], front)
    back = jnp.where(c == 0, got_ref[1], got_ref[0])
    part = n // lanes
    share = columns // lanes
    for i in range(lanes):
        o_ref[i, :part] = g_ref[i * part : (i + 1) * part]
        o_ref[i, part:] = jnp.where(owned(prow, c * lanes + i, share), back, front)


def message_of(at, prow, g, got, columns, lanes):
    n = g.shape[0]
    out = (lanes, n // lanes + got.shape[1], n)
    return pl.pallas_call(
        functools.partial(message_kernel, columns),
        out_shape=jax.ShapeDtypeStruct(out, f32),
        grid_spec=pltpu.PrefetchScalarGridSpec(
            num_scalar_prefetch=1,
            grid=(1,),
            in_specs=[held()] * 3,
            out_specs=whole(out),
        ),
        name="message",
    )(at, prow, g, in_vmem(got))


def half_kernel(part, keep_ref, sent_ref, got_ref, o_ref, line_ref):
    chips, half, lanes = keep_ref.shape
    peers, _, n = got_ref.shape
    o_ref[:, :half, :] = keep_ref[...] + sent_ref[...]
    total = got_ref[0, :part]
    for s in range(1, peers):
        total = total + got_ref[s, :part]
    for s in range(chips):
        for t in range(n // lanes):
            o_ref[s, half + t * part : half + (t + 1) * part, :] = total[:, t * lanes : (t + 1) * lanes]

    for s in range(peers):
        line_ref[s * 8 : (s + 1) * 8, :] = got_ref[s, part : part + 8]
    for s in range(line_ref.shape[0] - 8 * peers):
        line_ref[8 * peers + s : 8 * peers + s + 1, :] = got_ref[s, part + 8 : part + 9]


def add_halves(keep, sent, got, rows):
    chips, half, lanes = keep.shape
    peers, _, n = got.shape
    part = n // peers
    tall = half + part * (n // lanes)
    return pl.pallas_call(
        functools.partial(half_kernel, part),
        out_shape=(
            jax.ShapeDtypeStruct((chips, tall, lanes), f32),
            jax.ShapeDtypeStruct((rows, n), f32),
        ),
        in_specs=[held()] * 3,
        name="half",
    )(keep, in_vmem(sent), in_vmem(got))


def total_kernel(r_ref, share_ref, o_ref):
    chips, half, _ = o_ref.shape
    extra = r_ref.shape[1] - half
    total = r_ref[0, :half]
    for s in range(1, chips):
        total = total + r_ref[s, :half]
    share_ref[:half, :] = total
    for s in range(chips):
        o_ref[s] = total
        share_ref[half + s * extra : half + (s + 1) * extra, :] = r_ref[s, half:]


def total_of(received, half):
    chips, tall, lanes = received.shape
    return pl.pallas_call(
        total_kernel,
        out_shape=(
            jax.ShapeDtypeStruct((half + chips * (tall - half), lanes), f32),
            jax.ShapeDtypeStruct((chips, half, lanes), f32),
        ),
        in_specs=[held()],
        name="total",
    )(in_vmem(received))


def product_kernel(at_ref, pcol_ref, a_ref, w_ref, g_ref, keep_ref, send_ref, r_ref, a_buf, a_sem, k_buf, k_sem, s_buf, s_sem):
    c, k = at_ref[0], at_ref[1]
    rows, columns = a_ref.shape
    blocks, _, tn = a_buf.shape
    n = pcol_ref.shape[0]
    half = n // 2
    lanes = keep_ref.shape[2]
    parts = tn // lanes
    each(blocks, lambda b: columns_of(a_ref, a_buf, a_sem, b).start())

    def out(buffer, ref, sems, b):
        return pltpu.make_async_copy(buffer.at[b], ref.at[pl.ds(b * parts, parts)], sems.at[b])

    def block(b):
        columns_of(a_ref, a_buf, a_sem, b).wait()
        start = c * columns + b * tn
        onehot = onehot_rows(pcol_ref[...], start, tn)
        stays = (jnp.max(onehot, axis=0, keepdims=True) == 0) & (start + iota((1, tn), 1) >= n)
        hi, lo = split(jnp.where(stays, a_buf[b], 0.0), 2)
        w = w_ref[...]
        onehot = onehot.astype(bf16)
        r_ref[...] = folded(dot(w, jnp.concatenate([hi, onehot], axis=0))) + dot(w[:n, :rows], lo)

        @pl.when((c == 0) & (b < n // tn))
        def _():
            r_ref[...] = g_ref[...]

        for s in range(parts):
            cut = slice(s * lanes, (s + 1) * lanes)
            k_buf[b, s] = r_ref[pl.ds(k * half, half), cut]
            s_buf[b, s] = r_ref[pl.ds((1 - k) * half, half), cut]
        out(k_buf, keep_ref, k_sem, b).start()
        out(s_buf, send_ref, s_sem, b).start()

    each(blocks, block)

    def finish(b):
        out(k_buf, keep_ref, k_sem, b).wait()
        out(s_buf, send_ref, s_sem, b).wait()

    each(blocks, finish)


def product(at, pcol, a, w, g, chips):
    _, columns = a.shape
    n = g.shape[0]
    lanes = columns // chips
    blocks = columns // n
    shape = (chips, n // 2, lanes)
    made = [pltpu.VMEM((blocks, chips // blocks, n // 2, lanes), f32), pltpu.SemaphoreType.DMA((blocks,))]
    return pl.pallas_call(
        product_kernel,
        out_shape=(jax.ShapeDtypeStruct(shape, f32),) * 2,
        grid_spec=pltpu.PrefetchScalarGridSpec(
            num_scalar_prefetch=1,
            grid=(1,),
            in_specs=[whole(pcol.shape), HBM, whole(w.shape), whole((n, n))],
            out_specs=(HBM,) * 2,
            scratch_shapes=[pltpu.VMEM((n, n), f32), *streams(a.shape, n), *made, *made],
        ),
        name="product",
    )(at, pcol, a, w, g)


def permute_kernel(at_ref, pcol_ref, a_ref, p_ref, d_ref, o_ref, a_buf, a_sem, o_buf, o_sem):
    c = at_ref[0]
    columns = a_ref.shape[1]
    blocks, _, tn = a_buf.shape
    n = pcol_ref.shape[0]
    each(blocks, lambda b: columns_of(a_ref, a_buf, a_sem, b).start())

    def block(b):
        columns_of(a_ref, a_buf, a_sem, b).wait()
        onehot = onehot_rows(pcol_ref[...], c * columns + b * tn, tn)
        here = jnp.max(onehot, axis=0, keepdims=True) > 0
        o_buf[b] = jnp.where(here, dot(d_ref[...], twice(onehot.astype(bf16))), a_buf[b])

        @pl.when((c == 0) & (b < n // tn))
        def _():
            o_buf[b] = p_ref[...]

        columns_to(o_buf, o_ref, o_sem, b).start()

    each(blocks, block)
    each(blocks, lambda b: columns_to(o_buf, o_ref, o_sem, b).wait())


def permute(at, pcol, a, p, d):
    rows, _ = a.shape
    n = p.shape[1]
    return pl.pallas_call(
        permute_kernel,
        out_shape=jax.ShapeDtypeStruct(a.shape, f32),
        grid_spec=pltpu.PrefetchScalarGridSpec(
            num_scalar_prefetch=1,
            grid=(1,),
            in_specs=[whole(pcol.shape), HBM, whole((rows, n)), whole(d.shape)],
            out_specs=HBM,
            scratch_shapes=[*streams(a.shape, n), *streams(a.shape, n)],
        ),
        name="permute",
    )(at, pcol, a, p, d)


def unit_inverse(block):
    nb = block.shape[0]
    wide = 2 * nb
    sub = 8
    eye = jnp.where(iota((nb, nb), 0) == iota((nb, nb), 1), 1.0, 0.0)
    full = jnp.concatenate([block, eye], axis=1)
    tiles = [full[i : i + sub] for i in range(0, nb, sub)]
    at = iota((sub, wide), 0)
    for i in range(len(tiles)):
        cols = [[jnp.broadcast_to(t[:, i * sub + q : i * sub + q + 1], (sub, wide)) for t in tiles[i:]] for q in range(sub)]
        for q in range(sub):
            pivot = cols[q][0][q : q + 1]
            rest = 1.0 / pivot
            mult = [m * rest for m in cols[q]]
            mult[0] = jnp.where(at > q, mult[0], 0.0)
            for later in cols[q + 1 :]:
                row = later[0][q : q + 1]
                for u, m in enumerate(mult):
                    later[u] = later[u] - m * row
            row = tiles[i][q : q + 1]
            for u, m in enumerate(mult):
                tiles[i + u] = tiles[i + u] - m * row
    done = jnp.concatenate(tiles, axis=0)
    diagonal = jnp.sum(jnp.where(iota((nb, wide), 0) == iota((nb, wide), 1), done, 0.0), axis=1, keepdims=True)
    return done[:, nb:] * lax.rsqrt(diagonal)


def factor_kernel(at_ref, mine_ref, other_ref, p_ref, inv_ref, b_ref, t_ref):
    k = at_ref[1]
    n = p_ref.shape[1]
    lanes = mine_ref.shape[1]
    nb = 64
    half = n // 2
    width = n // lanes
    part = 8
    for s in range(half // part):
        for t in range(width):
            low = half + (s * width + t) * part
            cols = slice(t * lanes, (t + 1) * lanes)
            t_ref[pl.ds((2 * s + k) * part, part), cols] = mine_ref[low : low + part, :]
            t_ref[pl.ds((2 * s + 1 - k) * part, part), cols] = other_ref[low : low + part, :]
    t_ref[:, n:] = jnp.where(iota((n, n), 0) == iota((n, n), 1), 1.0, 0.0)
    for s in range(0, n, nb):
        inv = unit_inverse(t_ref[s : s + nb, s : s + nb])
        y = dot(inv, t_ref[s : s + nb, :], NN, highest)
        inv_ref[s : s + nb, :] = y[:, n:]
        if s + nb < n:
            t_ref[s + nb :, :] = t_ref[s + nb :, :] - dot(y[:, s + nb : n], y, TN, highest)
    inverse = inv_ref[...]
    hi, lo = split(dot(p_ref[...], dot(inverse, inverse, TN, highest), NN, highest), 2)
    for s, part in enumerate((hi, hi, lo)):
        b_ref[:, s * n : (s + 1) * n] = part


def factor(at, mine, other, p):
    rows, n = p.shape
    outs = (((n, n), f32), ((rows, 3 * n), bf16))
    return pl.pallas_call(
        factor_kernel,
        out_shape=tuple(jax.ShapeDtypeStruct(s, t) for s, t in outs),
        grid_spec=pltpu.PrefetchScalarGridSpec(
            num_scalar_prefetch=1,
            grid=(1,),
            in_specs=[held()] * 3,
            out_specs=tuple(whole(s) for s, _ in outs),
            scratch_shapes=[pltpu.VMEM((n, 2 * n), f32)],
        ),
        name="factor",
    )(at, mine, in_vmem(other), p)


def sketch_kernel(columns, at_ref, prow_ref, slots_ref, sk_ref, f_ref, o_ref):
    n = prow_ref.shape[1]
    pieces, _ = sk_ref.shape
    start = at_ref[0] * columns + at_ref[2] * pieces
    prow = prow_ref[...]
    place = start + iota((pieces, 1), 0)
    hit = jnp.where(place == prow, 1.0, 0.0)
    stays = (jnp.max(hit, axis=1, keepdims=True) == 0) & (place >= n)
    old = sk_ref[...]
    slots = slots_ref[...]
    own = (prow >= start) & (prow < start + pieces)
    f_ref[...] = jnp.where(own, dot(old, hit, TN, highest), slots)
    o_ref[...] = jnp.where(stays, old, 0.0) + dot(jnp.where(place >= n, hit, 0.0), slots, NT, highest)


def swap_sketch(at, prow, slots, sketch, columns):
    n = prow.shape[1]
    outs = ((sketch.shape[1], n), sketch.shape)
    return pl.pallas_call(
        functools.partial(sketch_kernel, columns),
        out_shape=tuple(jax.ShapeDtypeStruct(s, f32) for s in outs),
        grid_spec=pltpu.PrefetchScalarGridSpec(
            num_scalar_prefetch=1,
            grid=(1,),
            in_specs=[whole(v.shape) for v in (prow, slots, sketch)],
            out_specs=tuple(whole(s) for s in outs),
        ),
        name="sketch",
    )(at, prow, slots, sketch)


def share_kernel(columns, at_ref, mine_ref, other_ref, inv_ref, fronts_ref, sk_ref, u_ref, o_ref, s_ref, t_ref):
    c, k, r = at_ref[0], at_ref[1], at_ref[2]
    n = inv_ref.shape[0]
    half = n // 2
    pieces, _ = sk_ref.shape
    s_ref[pl.ds(k * half, half), :] = mine_ref[:half]
    s_ref[pl.ds((1 - k) * half, half), :] = other_ref[:half]
    t_ref[...] = s_ref[...].T
    inverse = inv_ref[...]
    upper = dot(t_ref[pl.ds(k * pieces, pieces), :], inverse, NT, highest)
    u_ref[...] = upper
    solved = dot(upper, inverse, NN, highest)
    place = c * columns + r * pieces + iota((pieces, 1), 0)
    lead = jnp.where(place == iota((1, n), 1), 1.0, 0.0)
    o_ref[...] = sk_ref[...] + dot(lead - solved, fronts_ref[...], NT, highest)


def finish_share(at, mine, other, inverse, fronts, sketch, columns):
    n = inverse.shape[0]
    outs = ((sketch.shape[0], n), sketch.shape)
    return pl.pallas_call(
        functools.partial(share_kernel, columns),
        out_shape=tuple(jax.ShapeDtypeStruct(s, f32) for s in outs),
        grid_spec=pltpu.PrefetchScalarGridSpec(
            num_scalar_prefetch=1,
            grid=(1,),
            in_specs=[held()] * 5,
            out_specs=tuple(whole(s) for s in outs),
            scratch_shapes=[pltpu.VMEM((n, mine.shape[1]), f32), pltpu.VMEM((mine.shape[1], n), f32)],
        ),
        name="share",
    )(at, mine, in_vmem(other), inverse, in_vmem(fronts), in_vmem(sketch))


def trailing_kernel(at_ref, a_ref, b_ref, mine_ref, other_ref, o_ref, s_ref, a_buf, a_sem, o_buf, o_sem):
    k = at_ref[1]
    _, half, lanes = mine_ref.shape
    blocks, _, tn = a_buf.shape
    parts = tn // lanes
    each(blocks, lambda b: columns_of(a_ref, a_buf, a_sem, b).start())

    def block(b):
        for s in range(parts):
            cut = slice(s * lanes, (s + 1) * lanes)
            s_ref[pl.ds(k * half, half), cut] = mine_ref[b * parts + s]
            s_ref[pl.ds((1 - k) * half, half), cut] = other_ref[b * parts + s]
        hi, lo = split(s_ref[...], 2)
        columns_of(a_ref, a_buf, a_sem, b).wait()
        o_buf[b] = a_buf[b] - dot(b_ref[...], jnp.concatenate([hi, lo, hi], axis=0))
        columns_to(o_buf, o_ref, o_sem, b).start()

    each(blocks, block)
    each(blocks, lambda b: columns_to(o_buf, o_ref, o_sem, b).wait())


def trail(at, a, b, mine, other):
    n = 2 * mine.shape[1]
    return pl.pallas_call(
        trailing_kernel,
        out_shape=jax.ShapeDtypeStruct(a.shape, f32),
        grid_spec=pltpu.PrefetchScalarGridSpec(
            num_scalar_prefetch=1,
            grid=(1,),
            in_specs=[HBM, whole(b.shape), held(), held()],
            out_specs=HBM,
            scratch_shapes=[pltpu.VMEM((n, n), f32), *streams(a.shape, n), *streams(a.shape, n)],
        ),
        name="trailing",
    )(at, a, b, in_vmem(mine), in_vmem(other))


def exchange(pieces, axis):
    return lax.all_to_all(pieces, axis, split_axis=0, concat_axis=0, tiled=True)


def to_all(piece, axis):
    return exchange(jnp.broadcast_to(piece[None], (lax.axis_size(axis), *piece.shape)), axis)


def side_of(value, which, dim):
    return lax.dynamic_index_in_dim(value, which, dim, keepdims=False)


def halved(value, which, axis, swap, dim):
    size = value.shape[dim] // 2
    value = value.reshape(*value.shape[:dim], 2, size, *value.shape[dim + 1 :])
    return side_of(value, which, dim) + lax.ppermute(side_of(value, 1 - which, dim), axis, swap)


def sum_at_rows(value):
    y, x, k = (lax.axis_index(a) for a in ROW)
    value = value.reshape(4, 4, 2, *value.shape[1:])
    near, far = [(0, 1), (1, 0), (2, 3), (3, 2)], [(0, 3), (3, 0), (1, 2), (2, 1)]
    value = halved(value, k, "row_2", [(0, 1), (1, 0)], 2)[:, :, 0]
    value = halved(value, x >> 1, "row_1", far, 1)
    value = halved(value, x & 1, "row_1", near, 1)[:, 0]
    value = halved(value, y >> 1, "row_0", far, 0)
    return halved(value, y & 1, "row_0", near, 0)[0]


def per_device(matrix, pivots, sketch):
    c = lax.axis_index("col")
    r = lax.axis_index(ROW)
    k = lax.axis_index("row_2")
    cols, lanes, chips = lax.axis_size("col"), lax.axis_size(ROW), lax.axis_size(CHIPS)
    rows, columns = matrix.shape
    n = pivots.shape[0]
    prow = pivots.reshape(1, n)
    at = scalars(c, k, r)
    swap = [(0, 1), (1, 0)]

    turned = sketch.T
    first = lax.ppermute(turned, "col", [(i, (i + 1) % cols) for i in range(cols)])
    mine, partner, pcol = extract(at, prow, matrix)
    arrived = exchange(mine.reshape(cols, rows // cols, n), "col")
    picks = pick_sketch(at, prow, partner, turned, first, columns, lanes)
    line = sum_at_rows(picks)
    inside = inside_of(at, prow, partner, matrix)
    message = holder(prow, arrived, columns)
    x = exchange(message, "col").reshape(rows, n)
    got = to_all(line, "col")
    panel, displaced, w, gram_part = gram(at, prow, x, mine, inside, columns)
    message = message_of(at, prow, gram_part, got, columns, lanes)
    gram_pieces = exchange(message, ROW)
    keep, send = product(at, pcol, matrix, w, gram_part, chips)
    sent = lax.ppermute(send, "row_2", swap)
    half, slots = add_halves(keep, sent, gram_pieces, sketch.shape[0])
    summands = exchange(half, CHIPS)
    permuted = permute(at, pcol, matrix, panel, displaced)
    fronts, swapped = swap_sketch(at, prow, slots, turned, columns)
    share, message = total_of(summands, n // 2)
    own_all = exchange(message, CHIPS)
    share_other = lax.ppermute(share, "row_2", swap)
    inverse, basis = factor(at, share, share_other, panel)
    upper_share, new_sketch = finish_share(at, share, share_other, inverse, fronts, swapped, columns)
    other_all = lax.ppermute(own_all, "row_2", swap)
    trailing = trail(at, permuted, basis, own_all, other_all)
    return (upper_share.T, trailing, new_sketch.T)


def solution(mesh):
    finer = Mesh(mesh.devices.reshape(4, 4, 2, mesh.shape["col"]), ("row_0", "row_1", "row_2", "col"))
    return jax.shard_map(
        per_device,
        mesh=finer,
        in_specs=(P(ROW, "col"), P(), P(None, COL_ROW)),
        out_specs=(P(None, COL_ROW), P(ROW, "col"), P(None, COL_ROW)),
        check_vma=False,
    )
```
